256 devices in a mesh: ens: 2 (over x_hi), lat: 4 (over x_lo, core), lon: 32 (over y, z).
Axes of the slice: x: 4 (x_hi: 2, x_lo: 2; x = x_hi * 2 + x_lo), y: 4, z: 8, core: 2. Of those that a mesh axis runs over, the one named last changes fastest.
Arguments:
- members_in: bfloat16 [8, 32, 512, 256], P('ens', 'lat', 'lon'), may hold values from -6 to 6
- out_grad: bfloat16 [8, 32, 512, 256], P('ens', 'lat', 'lon'), may hold values from -6 to 6
- weight: bfloat16 [9, 256, 256], replicated, may hold values from -0.125 to 0.125
- basis_blocks: float32 [8, 9, 3, 9], replicated, may hold values from -1.75 to 1.75
- cycle_block: int32 [32], replicated, may hold values from 0 to 7
- half_width: int32 [32, 3], replicated, may hold values from 1 to 4
Outputs:
- result: bfloat16 [8, 32, 512, 256], P('ens', 'lat', 'lon')
- in_grad: bfloat16 [8, 32, 512, 256], P('ens', 'lat', 'lon')
- weight_grad: float32 [9, 256, 256], P(None, 'lon')
The draws below stay inside these ranges and needn't reach their ends.
All inputs are finite; a program needn't handle non-finite values.
Results may differ from the reference program's by a relative error of at most 0.015.
Values may be sent and summed in bfloat16 or wider, within the bound.
No kernel may reach another device: no remote copies, remote signals or barrier semaphores. Data moves between devices by JAX's collectives and lax.ppermute only.
A program may use at most 64 MiB of HBM per device.

```python
import math
import jax
import jax.numpy as jnp
from jax import lax

C = 256
K = 9
R = 1
H = 4
NB = 8
MEMBERS = 8
NLAT = 32
NLON = 512


def draw_cycle_block(key, part):
    cycle_ids = jax.random.randint(jax.random.fold_in(key, 11), (NLAT,), 0, NB)
    order_ids = jax.random.permutation(jax.random.fold_in(key, 12), NB).astype(jnp.int32)
    return cycle_ids.astype(jnp.int32).at[:NB].set(order_ids)


def draw_half_width(key, part):
    cycle_ids = jnp.arange(NLAT, dtype=jnp.int32)
    distance = jnp.minimum(cycle_ids, NLAT - 1 - cycle_ids)
    spread = max(NLAT // 2, 1)
    baseline = H - 2 * distance * H // spread
    jitter = jax.random.randint(jax.random.fold_in(key, 21), (NLAT, 2 * R + 1), 0, 2)
    widths = jnp.clip(baseline[:, None] + jitter, 1, H)
    widths = widths.at[0].set(H).at[NLAT - 1].set(H).at[NLAT // 2].set(1)
    return widths.astype(jnp.int32)


def levels(stream_key, extent, split, least, high):
    def one(dim, blocks):
        steps = jax.random.uniform(jax.random.fold_in(jax.random.fold_in(stream_key, 6), dim), (blocks,), jnp.float32, least / len(split), high / len(split))
        return jnp.repeat(jnp.exp(steps), extent[dim] // blocks).reshape((-1,) + (1,) * (len(extent) - dim - 1))

    loudness = one(*split[0])
    for cut in split[1:]:
        loudness = loudness * one(*cut)
    return loudness


def scatter_about(stream_key, shape, scale, reach, split=(), held_as=jnp.bfloat16):
    drawn = scale * jax.random.normal(stream_key, shape, jnp.float32)
    if split:
        drawn = drawn * levels(stream_key, shape, split, -0.22, 0.18)
    return jnp.clip(drawn, -reach, reach).astype(held_as)


def setup_inputs(seed: int = 0) -> dict:
    splits = jax.random.split(jax.random.key(seed), 7)
    members_in = scatter_about(splits[0], (MEMBERS, NLAT, NLON, C), 1.0, 6.0, ((0, 2), (1, 4), (2, 32)))
    out_grad = scatter_about(splits[1], (MEMBERS, NLAT, NLON, C), 1.0, 6.0, ((0, 2), (1, 4), (2, 32)))
    weight = scatter_about(splits[2], (K, C, C), (K * C) ** -0.5, 0.125)
    basis_blocks = scatter_about(splits[3], (NB, K, 2 * R + 1, 2 * H + 1), ((2 * R + 1) * H) ** -0.5, 1.75, (), jnp.float32)
    cycle_block = draw_cycle_block(jax.random.fold_in(splits[6], 71), 0)
    half_width = draw_half_width(jax.random.fold_in(splits[6], 71), 0)
    return dict(members_in=members_in, out_grad=out_grad, weight=weight, basis_blocks=basis_blocks, cycle_block=cycle_block, half_width=half_width)


def filter_table(basis_blocks, cycle_block, half_width):
    picked = basis_blocks[cycle_block]
    offsets = jnp.arange(2 * H + 1, dtype=jnp.int32) - H
    inside = jnp.abs(offsets)[None, None, :] <= half_width[:, :, None]
    return jnp.where(inside[:, None, :, :], picked, jnp.float32(0.0))

def stencil(values, coefficients):
    padded = jnp.pad(values, ((R, R), (0, 0), (0, 0)))
    summed = jnp.zeros((NLAT, NLON, K, C), jnp.float32)
    for offset_row in range(2 * R + 1):
        strip_rows = padded[offset_row:offset_row + NLAT].astype(jnp.float32)
        for offset_col in range(2 * H + 1):
            rolled = jnp.roll(strip_rows, H - offset_col, axis=1)
            summed = summed + coefficients[:, None, :, offset_row, offset_col, None] * rolled[:, :, None, :]
    return summed.astype(jnp.bfloat16)

def adjoint(values, coefficients):
    padded = jnp.pad(values, ((R, R), (0, 0), (0, 0)))
    wide_table = jnp.pad(coefficients, ((R, R), (0, 0), (0, 0), (0, 0)), mode='edge')
    summed = jnp.zeros((NLAT, NLON, K, C), jnp.float32)
    for offset_row in range(2 * R + 1):
        lead_row = 2 * R - offset_row
        strip_rows = padded[lead_row:lead_row + NLAT].astype(jnp.float32)
        rows_coef = wide_table[lead_row:lead_row + NLAT]
        for offset_col in range(2 * H + 1):
            rolled = jnp.roll(strip_rows, offset_col - H, axis=1)
            summed = summed + rows_coef[:, None, :, offset_row, offset_col, None] * rolled[:, :, None, :]
    return summed.astype(jnp.bfloat16)

def reference(members_in, out_grad, weight, basis_blocks, cycle_block, half_width):
    coefficients = filter_table(basis_blocks, cycle_block, half_width)
    flat_weight = weight.reshape(K * C, C)

    def single(running, member_pair):
        values, cotangent = member_pair
        features = stencil(values, coefficients)
        feature_rows = features.reshape(NLAT * NLON, K * C)
        mixed = jnp.dot(feature_rows, flat_weight, preferred_element_type=jnp.float32)
        activated, slope_fn = jax.vjp(jax.nn.gelu, mixed)
        cot_rows = cotangent.reshape(NLAT * NLON, C).astype(jnp.float32)
        output_rows = (values.reshape(NLAT * NLON, C).astype(jnp.float32) + activated).astype(jnp.bfloat16)
        grad_mixed = slope_fn(cot_rows)[0].astype(jnp.bfloat16)
        running = running + lax.dot_general(feature_rows, grad_mixed, (((0,), (0,)), ((), ())), preferred_element_type=jnp.float32)
        back = adjoint(grad_mixed.reshape(NLAT, NLON, C), coefficients)
        branch_rows = lax.dot_general(back.reshape(NLAT * NLON, K, C), weight, (((1, 2), (0, 2)), ((), ())), preferred_element_type=jnp.float32)
        grad_rows = (cot_rows + branch_rows).astype(jnp.bfloat16)
        return (running, (output_rows.reshape(NLAT, NLON, C), grad_rows.reshape(NLAT, NLON, C)))
    summed, (result, in_grad) = lax.scan(single, jnp.zeros((K * C, C), jnp.float32), (members_in, out_grad))
    weight_grad = (summed * (1.0 / math.sqrt(MEMBERS * NLAT * NLON))).reshape(K, C, C)
    return (result, in_grad, weight_grad)
```

```python
import math

import jax
import jax.numpy as jnp
from jax import lax
from jax.sharding import PartitionSpec as P

C = 256
K = 9
R = 1
H = 4


def extended(block, sides, width, periodic):
    for axis, dim in sides:
        count = lax.axis_size(axis)
        forward = [(i, i + 1) for i in range(count - 1)]
        if periodic:
            forward.append((count - 1, 0))
        backward = [(target, source) for source, target in forward]
        low = lax.ppermute(
            lax.slice_in_dim(block, block.shape[dim] - width, None, axis=dim), axis, forward
        )
        high = lax.ppermute(lax.slice_in_dim(block, 0, width, axis=dim), axis, backward)
        block = jnp.concatenate([low, block, high], axis=dim)
    return block


def local_table(basis_blocks, cycle_block, half_width, first_cycle, cycle_count):
    total_cycles = cycle_block.shape[0]
    cycle_ids = jnp.clip(
        first_cycle + jnp.arange(cycle_count, dtype=jnp.int32), 0, total_cycles - 1
    )
    one_hot = (cycle_ids[:, None] == jnp.arange(total_cycles, dtype=jnp.int32)[None, :]).astype(
        jnp.int32
    )
    block_ids = jnp.sum(one_hot * cycle_block[None, :], axis=1)
    widths = jnp.sum(one_hot[:, :, None] * half_width[None, :, :], axis=1)
    block_count = basis_blocks.shape[0]
    pick_block = (block_ids[:, None] == jnp.arange(block_count, dtype=jnp.int32)[None, :]).astype(
        jnp.float32
    )
    picked = jnp.dot(
        pick_block,
        basis_blocks.reshape(block_count, -1),
        precision=lax.Precision.HIGHEST,
        preferred_element_type=jnp.float32,
    )
    picked = picked.reshape((cycle_count,) + basis_blocks.shape[1:])
    offsets = jnp.arange(2 * H + 1, dtype=jnp.int32) - H
    inside = jnp.abs(offsets)[None, None, :] <= widths[:, :, None]
    return (jnp.where(inside[:, None, :, :], picked, jnp.float32(0.0)), widths)


def extend(values):
    tall_block = extended(values, (("lat", 1),), R, False)
    return extended(tall_block, (("lon", 2),), H, True)


def spread_forward(padded, coefficients, half_reach):
    lat_rows = padded.shape[1] - 2 * R
    lon_cols = padded.shape[2] - 2 * H

    def single(member):
        summed = jnp.zeros(
            (lat_rows, lon_cols, coefficients.shape[1], member.shape[-1]), jnp.float32
        )
        for offset_row in range(2 * R + 1):
            for offset_col in range(H - half_reach, H + half_reach + 1):
                sliced = member[
                    offset_row : offset_row + lat_rows, offset_col : offset_col + lon_cols
                ]
                summed = summed + coefficients[:, None, :, offset_row, offset_col, None] * sliced[
                    :, :, None, :
                ].astype(jnp.float32)
        return summed.astype(jnp.bfloat16)

    return lax.map(single, padded)


def spread_adjoint(padded, coefficients, half_reach):
    lat_rows = padded.shape[1] - 2 * R
    lon_cols = padded.shape[2] - 2 * H

    def single(member):
        summed = jnp.zeros(
            (lat_rows, lon_cols, coefficients.shape[1], member.shape[-1]), jnp.float32
        )
        for offset_row in range(2 * R + 1):
            lead_row = 2 * R - offset_row
            rows_coef = coefficients[lead_row : lead_row + lat_rows]
            for offset_col in range(H - half_reach, H + half_reach + 1):
                lead_col = 2 * H - offset_col
                sliced = member[lead_row : lead_row + lat_rows, lead_col : lead_col + lon_cols]
                summed = summed + rows_coef[:, None, :, offset_row, offset_col, None] * sliced[
                    :, :, None, :
                ].astype(jnp.float32)
        return summed.astype(jnp.bfloat16)

    return lax.map(single, padded)


def apply_spread(kernel, padded, coefficients):
    return kernel(padded, coefficients, H)


CORES = 2
YS = 4
ZS = 8
XS = 4


def core_swap():
    return [(i, i ^ 1) for i in range(4)]


def y_shift(step):
    return [(y * ZS + z, ((y + step) % YS) * ZS + z) for y in range(YS) for z in range(ZS)]


def x_shift(step):
    return [(i, (i + CORES * step) % (XS * CORES)) for i in range(XS * CORES)]


def reduce_gradient(local_grad):
    half = C // CORES
    rows = C // YS
    core = lax.rem(lax.axis_index("lat"), CORES)
    x_index = lax.axis_index("ens") * 2 + lax.axis_index("lat") // CORES
    y_index = lax.axis_index("lon") // ZS
    halves = local_grad.reshape(K, C, CORES, half).transpose(2, 1, 0, 3).reshape(CORES, C, K * half)
    mine = lax.dynamic_index_in_dim(halves, core, 0, keepdims=False)
    other = lax.dynamic_index_in_dim(halves, 1 - core, 0, keepdims=False)
    got = lax.ppermute(other.astype(jnp.bfloat16), "lat", core_swap())
    blocks = (mine + got.astype(jnp.float32)).reshape(YS, rows, K * half)
    total = lax.dynamic_index_in_dim(blocks, y_index, 0, keepdims=False)
    for step in range(1, YS):
        sent = lax.dynamic_index_in_dim(
            blocks, lax.rem(y_index + step, YS), 0, keepdims=False
        ).astype(jnp.bfloat16)
        total = total + lax.ppermute(sent, "lon", y_shift(step)).astype(jnp.float32)
    groups = [[y * ZS + z for z in range(ZS)] for y in range(YS)]
    shares = lax.all_to_all(
        total.astype(jnp.bfloat16).reshape(ZS, rows // ZS, K * half),
        "lon",
        0,
        0,
        axis_index_groups=groups,
        tiled=True,
    )
    share = jnp.sum(shares.astype(jnp.float32), axis=0).astype(jnp.bfloat16)
    held = [share] + [
        lax.ppermute(share, ("ens", "lat"), x_shift(step)) for step in range(1, XS)
    ]
    held = jnp.stack(held).astype(jnp.float32)
    total = jnp.zeros(share.shape, jnp.float32)
    for source in range(XS):
        total = total + lax.dynamic_index_in_dim(
            held, lax.rem(x_index - source + XS, XS), 0, keepdims=False
        )
    other = lax.ppermute(total, "lat", core_swap())
    low = jnp.where(core == 0, total, other).reshape(-1, K, half)
    high = jnp.where(core == 0, other, total).reshape(-1, K, half)
    return jnp.concatenate([low, high], axis=2).transpose(1, 0, 2)


def shards(members_in, out_grad, weight, basis_blocks, cycle_block, half_width):
    members, lat_rows, lon_cols, channels = members_in.shape
    first_cycle = lax.axis_index("lat") * lat_rows
    wide_coef, wide_widths = local_table(
        basis_blocks, cycle_block, half_width, first_cycle - R, lat_rows + 2 * R
    )
    own_coef = wide_coef[R : R + lat_rows]
    padded_in = extend(members_in)
    features = apply_spread(spread_forward, padded_in, own_coef)
    feature_rows = features.reshape(members * lat_rows * lon_cols, K * C)
    mixed = jnp.dot(feature_rows, weight.reshape(K * C, C), preferred_element_type=jnp.float32)
    activated, slope_fn = jax.vjp(jax.nn.gelu, mixed)
    cot_rows = out_grad.reshape(-1, channels).astype(jnp.float32)
    result = (members_in.reshape(-1, channels).astype(jnp.float32) + activated).astype(jnp.bfloat16)
    grad_mixed = slope_fn(cot_rows)[0].astype(jnp.bfloat16)
    cell_count = (
        members
        * lax.axis_size("ens")
        * lat_rows
        * lax.axis_size("lat")
        * lon_cols
        * lax.axis_size("lon")
    )
    local_grad = lax.dot_general(
        feature_rows, grad_mixed, (((0,), (0,)), ((), ())), preferred_element_type=jnp.float32
    )
    local_grad = (local_grad * (1.0 / math.sqrt(cell_count))).reshape(K, C, C)
    weight_grad = reduce_gradient(local_grad)
    padded_grad = extend(grad_mixed.reshape(members, lat_rows, lon_cols, channels))
    back = apply_spread(spread_adjoint, padded_grad, wide_coef)
    branch_rows = lax.dot_general(
        back.reshape(-1, K, C),
        weight,
        (((1, 2), (0, 2)), ((), ())),
        preferred_element_type=jnp.float32,
    )
    in_grad = (cot_rows + branch_rows).astype(jnp.bfloat16)
    return (result.reshape(members_in.shape), in_grad.reshape(members_in.shape), weight_grad)


def solution(mesh):
    return jax.shard_map(
        shards,
        mesh=mesh,
        in_specs=(P("ens", "lat", "lon", None), P("ens", "lat", "lon", None), P(), P(), P(), P()),
        out_specs=(
            P("ens", "lat", "lon", None),
            P("ens", "lat", "lon", None),
            P(None, "lon", None),
        ),
        check_vma=False,
    )
```

```python
import functools
import math

import jax
import jax.numpy as jnp
from jax import lax
from jax.experimental import pallas as pl
from jax.experimental.pallas import tpu as pltpu
from jax.sharding import PartitionSpec as P

C = 256
K = 9
R = 1
H = 4
TAPS = 2 * H + 1

CORES = 2
YS = 4
ZS = 8
XS = 4

M = 4
ROWS = 8
COLS = 16
WIDE = COLS + 4 * H
MID = COLS + 2 * H
X_ROWS = ROWS + 4 * R
G_ROWS = ROWS + 2 * R
G_PAD = G_ROWS * MID + 32
BF = jnp.bfloat16
F32 = jnp.float32


def core_swap():
    return [(i, i ^ 1) for i in range(4)]


def y_shift(step):
    return [(y * ZS + z, ((y + step) % YS) * ZS + z) for y in range(YS) for z in range(ZS)]


def fold_kernel(y, mine, got, own, *sent):
    rows = C // YS
    for step in range(YS):
        at = pl.multiple_of(lax.rem(y[0] + step, YS) * rows, rows)
        total = mine[pl.ds(at, rows), :].astype(F32) + got[pl.ds(at, rows), :].astype(F32)
        if step == 0:
            own[...] = total
        else:
            sent[step - 1][...] = total.astype(BF)


def join_kernel(own, one, two, three, out):
    total = own[...] + one[...].astype(F32) + two[...].astype(F32) + three[...].astype(F32)
    out[...] = total.reshape(out.shape).astype(BF)


def share_kernel(shares, out):
    total = shares[0].astype(F32)
    for z in range(1, ZS):
        total = total + shares[z].astype(F32)
    for copy in range(XS * CORES):
        out[copy] = total.astype(BF)


def place_kernel(shares, out):
    half = C // CORES
    for core in range(CORES):
        total = shares[core].astype(F32)
        for x in range(1, XS):
            total = total + shares[x * CORES + core].astype(F32)
        for k in range(K):
            out[k, :, core * half : (core + 1) * half] = total[:, k * half : (k + 1) * half]


def table_kernel(cycles, widths, first, basis, x, near, far, x_turned):
    lane = lax.broadcasted_iota(jnp.int32, (1, 128), 1)
    total = cycles.shape[0]
    blocks = []
    reach = []
    for row in range(G_ROWS):
        cycle = jnp.clip(first[0] + (row - R), 0, total - 1)
        blocks.append(cycles[cycle])
        reach.append([widths[r, cycle] for r in range(3)])
    for p in range(G_ROWS // 2):
        bases = []
        for row in (2 * p, 2 * p + 1):
            limit = jnp.where(
                lane < 32, reach[row][0], jnp.where(lane < 64, reach[row][1], reach[row][2])
            )
            inside = jnp.abs((lane & 31) - H) <= limit
            base = jnp.where(inside, basis[blocks[row], :, 0:128], 0.0)
            bases.append(pltpu.roll(base, 32, 1) if row % 2 else base)
        for k in range(K):
            bands = [
                pltpu.roll(
                    jnp.broadcast_to(base[k : k + 1], (MID, 128)), 0, 1, stride=1, stride_axis=0
                )
                for base in bases
            ]
            near[p, k] = jnp.concatenate(bands, axis=0).astype(BF)
    for row in range(ROWS):
        base = jnp.zeros((K, 128), F32)
        for t in range(3):
            place = lane - MID * t
            inside = (place >= 0) & (place < TAPS) & (jnp.abs(place - H) <= reach[row + t][2 - t])
            base = base + jnp.where(inside, basis[blocks[row + t], :, 128:256], 0.0)
        if row % 2:
            base = pltpu.roll(base, MID, 1)
        for k in range(K):
            band = pltpu.roll(
                jnp.broadcast_to(base[k : k + 1], (COLS, 128)), 0, 1, stride=1, stride_axis=0
            )
            far[row // 2, k, COLS * (row % 2) : COLS * (row % 2) + COLS] = band.astype(BF)
    for m in range(M):
        flat = x[m].reshape(ROWS * COLS, C).astype(F32)
        x_turned[:, m * ROWS * COLS : (m + 1) * ROWS * COLS] = flat.T.astype(BF)


def side_kernel(x_in, grad_in, left, right, x, grad, sems):
    copies = [
        pltpu.make_async_copy(x_in, x, sems.at[0]),
        pltpu.make_async_copy(grad_in, grad, sems.at[1]),
    ]
    for copy in copies:
        copy.start()
    copies[0].wait()

    def x_member(m, carry):
        for r in range(ROWS):
            row = x[m, r].astype(F32)
            left[m, r] = row[0:8].astype(BF)
            right[m, r] = row[8:16].astype(BF)
        return carry

    lax.fori_loop(0, M, x_member, 0)
    copies[1].wait()

    def g_member(m, carry):
        for q in range(ROWS // 2):
            one = grad[m, 2 * q].astype(F32)
            two = grad[m, 2 * q + 1].astype(F32)
            left[m, ROWS + q] = jnp.concatenate([one[0:4], two[0:4]], axis=0).astype(BF)
            right[m, ROWS + q] = jnp.concatenate([one[12:16], two[12:16]], axis=0).astype(BF)
        return carry

    lax.fori_loop(0, M, g_member, 0)


def rim_rows(x, grad, left_x, right_x, left_g, right_g, at, out):
    def member(m, carry):
        for r in range(2):
            row = x[m, r].astype(F32)
            out[m, 4 * r] = left_x[m, r]
            out[m, 4 * r + 1] = row[0:8].astype(BF)
            out[m, 4 * r + 2] = row[8:16].astype(BF)
            out[m, 4 * r + 3] = right_x[m, r]
        before = left_g[m, 0].astype(F32)[at : at + 4]
        after = right_g[m, 0].astype(F32)[at : at + 4]
        line = jnp.concatenate([before, grad[m, 0].astype(F32), after], axis=0).astype(BF)
        for t in range(3):
            out[m, 8 + t] = line[8 * t : 8 * t + 8]
        return carry

    lax.fori_loop(0, M, member, 0)


def rim_kernel(*refs):
    rim_rows(*refs[0:6], 4, refs[12])
    rim_rows(*refs[6:12], 0, refs[13])


def adjoint_rows(far, grads, back):
    def member(m, carry):
        for p in range(ROWS // 2):
            spread = jnp.dot(
                far[p].reshape(K * 32, 128),
                grads[m, 2 * MID * p : 2 * MID * p + 128],
                preferred_element_type=F32,
            )
            start = pl.multiple_of(m * ROWS * COLS + 32 * p, 32)
            for k in range(K):
                back[pl.ds(start, 32), k * C : (k + 1) * C] = spread[32 * k : 32 * k + 32].astype(BF)
        return carry

    lax.fori_loop(0, M, member, 0)


def main_kernel(
    scale, core, x, x_turned, out_grad, weight, near, far, top_in, bottom_in, left_in, right_in,
    result, grads, mine, other,
    wide, cotangent, features, mixed, back, top, bottom, left, right, sems,
):
    copies = [
        pltpu.make_async_copy(source, target, sems.at[n])
        for n, (source, target) in enumerate(
            ((left_in, left), (right_in, right), (top_in, top), (bottom_in, bottom))
        )
    ]
    for copy in copies:
        copy.start()
    for copy in copies:
        copy.wait()

    def gather(m, carry):
        for r in range(2):
            for at, rim in ((r, top), (X_ROWS - 2 + r, bottom)):
                row = jnp.concatenate([rim[m, 4 * r + t].astype(F32) for t in range(4)], axis=0)
                wide[m, WIDE * at : WIDE * at + WIDE] = row.astype(BF)
        for at, rim in ((0, top), (G_ROWS - 1, bottom)):
            cotangent[m, MID * at : MID * at + MID] = jnp.concatenate(
                [rim[m, 8 + t].astype(F32) for t in range(3)], axis=0
            )
        for r in range(ROWS):
            row = jnp.concatenate(
                [left[m, r].astype(F32), x[m, r].astype(F32), right[m, r].astype(F32)], axis=0
            )
            wide[m, WIDE * (r + 2) : WIDE * (r + 2) + WIDE] = row.astype(BF)
            at = 4 * (r % 2)
            before = left[m, ROWS + r // 2].astype(F32)[at : at + 4]
            after = right[m, ROWS + r // 2].astype(F32)[at : at + 4]
            cotangent[m, MID * (r + 1) : MID * (r + 1) + MID] = jnp.concatenate(
                [before, out_grad[m, r].astype(F32), after], axis=0
            )
        for p in range(G_ROWS // 2):
            spread = jnp.dot(
                near[p].reshape(K * 2 * MID, 128),
                wide[m, 2 * WIDE * p : 2 * WIDE * p + 128],
                preferred_element_type=F32,
            )
            start = pl.multiple_of(m * G_ROWS * MID + 2 * MID * p, 16)
            for k in range(K):
                features[pl.ds(start, 2 * MID), k * C : (k + 1) * C] = spread[
                    2 * MID * k : 2 * MID * k + 2 * MID
                ].astype(BF)
        return carry

    lax.fori_loop(0, M, gather, 0)
    mixed[...] = jnp.dot(features[...], weight[...], preferred_element_type=F32).reshape(
        M, G_ROWS * MID, C
    )
    slope = math.sqrt(2.0 / math.pi)

    def activate(m, carry):
        for p in range(G_ROWS // 2):
            v = mixed[m, 2 * MID * p : 2 * MID * p + 2 * MID]
            square = v * v
            t = jnp.tanh(slope * v * (1.0 + 0.044715 * square))
            half = 0.5 * (1.0 + t)
            rise = half + 0.5 * v * (1.0 - t * t) * (slope * (1.0 + 3 * 0.044715 * square))
            grad = cotangent[m, 2 * MID * p : 2 * MID * p + 2 * MID] * rise
            grads[m, 2 * MID * p : 2 * MID * p + 2 * MID] = grad.astype(BF)
            act = v * half
            for part in range(2):
                r = 2 * p + part - R
                if 0 <= r < ROWS:
                    own = act[MID * part + H : MID * part + H + COLS]
                    result[m, r] = (x[m, r].astype(F32) + own).astype(BF)
        grads[m, G_ROWS * MID : G_PAD] = jnp.zeros((G_PAD - G_ROWS * MID, C), BF)
        return carry

    lax.fori_loop(0, M, activate, 0)
    adjoint_rows(far, grads, back)
    first = core[0] == 0
    for k in range(K):
        part = scale * jnp.dot(
            x_turned[...], back[:, k * C : (k + 1) * C], preferred_element_type=F32
        )
        low = part[:, 0:128]
        high = part[:, 128:256]
        mine[:, 128 * k : 128 * k + 128] = jnp.where(first, low, high).astype(BF)
        other[:, 128 * k : 128 * k + 128] = jnp.where(first, high, low).astype(BF)


def tail_kernel(grads, out_grad, weight, far, tie, in_grad, tied, back):
    adjoint_rows(far, grads, back)
    total = out_grad[...].reshape(M * ROWS * COLS, C).astype(F32)
    for k in range(K):
        total = total + lax.dot_general(
            back[:, k * C : (k + 1) * C],
            weight[k],
            (((1,), (1,)), ((), ())),
            preferred_element_type=F32,
        )
    in_grad[...] = total.reshape(M, ROWS, COLS, C).astype(BF)


VM = pl.BlockSpec(memory_space=pltpu.VMEM)
SM = pl.BlockSpec(memory_space=pltpu.SMEM)
KEPT = pl.BlockSpec(memory_space=pl.ANY)
FAR = pl.BlockSpec(memory_space=pltpu.HBM)


def call(kernel, ins, outs, args, name, scratch=(), mib=8, flops=0, moved=1 << 20, tie=None, sems=0):
    aliases = {}
    out_specs = [VM] * len(outs)
    outs = [jax.ShapeDtypeStruct(*o) for o in outs]
    if tie is not None:
        aliases = {len(args): len(outs)}
        ins = ins + [KEPT]
        args = args + (tie,)
        out_specs = out_specs + [KEPT]
        outs = outs + [jax.ShapeDtypeStruct(tie.shape, tie.dtype)]
    return pl.pallas_call(
        kernel,
        out_shape=outs,
        in_specs=ins,
        out_specs=out_specs,
        scratch_shapes=[pltpu.VMEM(*s) for s in scratch]
        + [pltpu.SemaphoreType.DMA((sems,))] * (sems > 0),
        input_output_aliases=aliases,
        cost_estimate=pl.CostEstimate(flops=flops, bytes_accessed=moved, transcendentals=0),
        compiler_params=pltpu.CompilerParams(vmem_limit_bytes=mib << 20),
        name=name,
    )(*args)


def edge(rows, block, width):
    return pl.BlockSpec((M, rows, width, C), lambda i: (0, block, 0, 0))


def send_sides(x, out_grad):
    shape = (M, ROWS + ROWS // 2, 8, C)
    to_left, to_right = call(
        side_kernel,
        [FAR] * 2,
        [(shape, BF)] * 2,
        (x, out_grad),
        "side",
        scratch=[(x.shape, BF)] * 2,
        sems=2,
    )
    count = lax.axis_size("lon")
    left = lax.ppermute(to_right, "lon", [(i, (i + 1) % count) for i in range(count)])
    right = lax.ppermute(to_left, "lon", [((i + 1) % count, i) for i in range(count)])
    return left, right


def send_rims(x, out_grad, left, right):
    shape = (M, 11, 8, C)
    whole = pl.BlockSpec(shape, lambda i: (0, 0, 0, 0))
    ins = []
    for x_at, g_at in ((ROWS // 2 - 1, ROWS - 1), (0, 0)):
        ins += [edge(2, x_at, COLS), edge(1, g_at, COLS)]
        ins += [edge(2, x_at, 8)] * 2 + [edge(1, ROWS + g_at // 2, 8)] * 2
    up, down = pl.pallas_call(
        rim_kernel,
        grid=(1,),
        out_shape=[jax.ShapeDtypeStruct(shape, BF)] * 2,
        in_specs=ins,
        out_specs=[whole] * 2,
        cost_estimate=pl.CostEstimate(flops=0, bytes_accessed=1 << 18, transcendentals=0),
        compiler_params=pltpu.CompilerParams(vmem_limit_bytes=6 << 20),
        name="rim",
    )(*((x, out_grad, left, right, left, right) * 2))
    count = lax.axis_size("lat")
    top = lax.ppermute(up, "lat", [(i, i + 1) for i in range(count - 1)])
    bottom = lax.ppermute(down, "lat", [(i + 1, i) for i in range(count - 1)])
    return top, bottom


def reduce_gradient(mine, other, behind):
    half = K * C // CORES
    rows = C // YS
    share_rows = rows // ZS
    y_index = (lax.axis_index("lon") // ZS).reshape(1)
    got = lax.ppermute(other, "lat", core_swap())
    own, *sent = call(
        fold_kernel,
        [SM, VM, VM],
        [((rows, half), F32)] + [((rows, half), BF)] * 3,
        (y_index, mine, got),
        "fold",
    )
    parts = [lax.ppermute(sent[step - 1], "lon", y_shift(step)) for step in range(1, YS)]
    extra, own = behind(own)
    (joined,) = call(
        join_kernel, [VM] * 4, [((ZS, share_rows, half), BF)], (own, *parts), "join"
    )
    groups = [[y * ZS + z for z in range(ZS)] for y in range(YS)]
    shares = lax.all_to_all(joined, "lon", 0, 0, axis_index_groups=groups, tiled=True)
    (share,) = call(
        share_kernel, [VM], [((XS * CORES, share_rows, half), BF)], (shares,), "share"
    )
    shares = lax.all_to_all(share, ("ens", "lat"), 0, 0, tiled=True)
    (weight_grad,) = call(place_kernel, [VM], [((K, share_rows, C), F32)], (shares,), "place")
    return weight_grad, extra


def shards(members_in, out_grad, weight, basis_blocks, cycle_block, half_width):
    lat = lax.axis_index("lat")
    left, right = send_sides(members_in, out_grad)
    blocks = basis_blocks.shape[0]
    basis = jnp.pad(basis_blocks, ((0, 0), (0, 0), (0, 0), (0, 32 - TAPS))).reshape(blocks, K, 96)
    flipped = jnp.pad(
        basis_blocks[:, :, ::-1, ::-1], ((0, 0), (0, 0), (0, 0), (0, MID - TAPS))
    ).reshape(blocks, K, 72)
    gap = jnp.zeros((blocks, K, 32), F32)
    basis = jnp.concatenate([basis, gap, flipped, gap, gap[:, :, :24]], axis=2)

    near, far, x_turned = call(
        table_kernel,
        [SM] * 3 + [VM] * 2,
        [
            ((G_ROWS // 2, K, 2 * MID, 128), BF),
            ((ROWS // 2, K, 32, 128), BF),
            ((C, M * ROWS * COLS), BF),
        ],
        (cycle_block, half_width.T, (lat * ROWS).reshape(1), basis, members_in),
        "table",
        flops=1 << 24,
        moved=3 << 20,
    )
    top, bottom = send_rims(members_in, out_grad, left, right)
    cell_count = (
        M * lax.axis_size("ens") * ROWS * lax.axis_size("lat") * COLS * lax.axis_size("lon")
    )
    half_shape = (C, K * C // CORES)
    result, grads, mine, other = call(
        functools.partial(main_kernel, 1.0 / math.sqrt(cell_count)),
        [SM] + [VM] * 6 + [FAR] * 4,
        [
            (members_in.shape, BF),
            ((M, G_PAD, C), BF),
            (half_shape, BF),
            (half_shape, BF),
        ],
        (
            lax.rem(lat, CORES).reshape(1),
            members_in,
            x_turned,
            out_grad,
            weight.reshape(K * C, C),
            near,
            far,
            top,
            bottom,
            left,
            right,
        ),
        "main",
        scratch=[
            ((M, X_ROWS * WIDE, C), BF),
            ((M, G_ROWS * MID, C), F32),
            ((M * G_ROWS * MID, K * C), BF),
            ((M, G_ROWS * MID, C), F32),
            ((M * ROWS * COLS, K * C), BF),
            (top.shape, BF),
            (bottom.shape, BF),
            (left.shape, BF),
            (right.shape, BF),
        ],
        sems=4,
        mib=32,
        flops=5 << 30,
        moved=8 << 20,
    )

    def tail(tie):
        return call(
            tail_kernel,
            [VM] * 4,
            [(members_in.shape, BF)],
            (grads, out_grad, weight, far),
            "tail",
            scratch=[((M * ROWS * COLS, K * C), BF)],
            mib=16,
            flops=2 << 30,
            moved=4 << 20,
            tie=tie,
        )

    weight_grad, in_grad = reduce_gradient(mine, other, tail)
    return (result, in_grad, weight_grad)


def solution(mesh):
    return jax.shard_map(
        shards,
        mesh=mesh,
        in_specs=(P("ens", "lat", "lon", None), P("ens", "lat", "lon", None), P(), P(), P(), P()),
        out_specs=(
            P("ens", "lat", "lon", None),
            P("ens", "lat", "lon", None),
            P(None, "lon", None),
        ),
        check_vma=False,
    )
```

```python
import functools
import math

import jax
import jax.numpy as jnp
from jax import lax
from jax.experimental import pallas as pl
from jax.experimental.pallas import tpu as pltpu
from jax.sharding import PartitionSpec as P

C = 256
K = 9
R = 1
H = 4
TAPS = 2 * H + 1

CORES = 2
YS = 4
ZS = 8
XS = 4

M = 4
ROWS = 8
COLS = 16
WIDE = COLS + 4 * H
MID = COLS + 2 * H
X_ROWS = ROWS + 4 * R
G_ROWS = ROWS + 2 * R
G_PAD = G_ROWS * MID + 32
BF = jnp.bfloat16
F32 = jnp.float32


def core_swap():
    return [(i, i ^ 1) for i in range(4)]


def y_shift(step):
    return [(y * ZS + z, ((y + step) % YS) * ZS + z) for y in range(YS) for z in range(ZS)]


def fold_kernel(y, mine, got, own, *sent):
    rows = C // YS
    for step in range(YS):
        at = pl.multiple_of(lax.rem(y[0] + step, YS) * rows, rows)
        total = mine[pl.ds(at, rows), :].astype(F32) + got[pl.ds(at, rows), :].astype(F32)
        if step == 0:
            own[...] = total
        else:
            sent[step - 1][...] = total.astype(BF)


def join_kernel(own, one, two, three, out):
    total = own[...] + one[...].astype(F32) + two[...].astype(F32) + three[...].astype(F32)
    out[...] = total.reshape(out.shape).astype(BF)


def share_kernel(shares, out):
    total = shares[0].astype(F32)
    for z in range(1, ZS):
        total = total + shares[z].astype(F32)
    for copy in range(XS * CORES):
        out[copy] = total.astype(BF)


def place_kernel(shares, out):
    half = C // CORES
    for core in range(CORES):
        total = shares[core].astype(F32)
        for x in range(1, XS):
            total = total + shares[x * CORES + core].astype(F32)
        for k in range(K):
            out[k, :, core * half : (core + 1) * half] = total[:, k * half : (k + 1) * half]


def table_kernel(cycles, widths, first, basis, x, near, far, x_turned):
    lane = lax.broadcasted_iota(jnp.int32, (1, 128), 1)
    total = cycles.shape[0]
    blocks = []
    reach = []
    for row in range(G_ROWS):
        cycle = jnp.clip(first[0] + (row - R), 0, total - 1)
        blocks.append(cycles[cycle])
        reach.append([widths[r, cycle] for r in range(3)])
    for p in range(G_ROWS // 2):
        bases = []
        for row in (2 * p, 2 * p + 1):
            limit = jnp.where(
                lane < 32, reach[row][0], jnp.where(lane < 64, reach[row][1], reach[row][2])
            )
            inside = jnp.abs((lane & 31) - H) <= limit
            base = jnp.where(inside, basis[blocks[row], :, 0:128], 0.0)
            bases.append(pltpu.roll(base, 32, 1) if row % 2 else base)
        for k in range(K):
            bands = [
                pltpu.roll(
                    jnp.broadcast_to(base[k : k + 1], (MID, 128)), 0, 1, stride=1, stride_axis=0
                )
                for base in bases
            ]
            near[p, k] = jnp.concatenate(bands, axis=0).astype(BF)
    for row in range(ROWS):
        base = jnp.zeros((K, 128), F32)
        for t in range(3):
            place = lane - MID * t
            inside = (place >= 0) & (place < TAPS) & (jnp.abs(place - H) <= reach[row + t][2 - t])
            base = base + jnp.where(inside, basis[blocks[row + t], :, 128:256], 0.0)
        if row % 2:
            base = pltpu.roll(base, MID, 1)
        for k in range(K):
            band = pltpu.roll(
                jnp.broadcast_to(base[k : k + 1], (COLS, 128)), 0, 1, stride=1, stride_axis=0
            )
            far[row // 2, k, COLS * (row % 2) : COLS * (row % 2) + COLS] = band.astype(BF)
    for m in range(M):
        flat = x[m].reshape(ROWS * COLS, C).astype(F32)
        x_turned[:, m * ROWS * COLS : (m + 1) * ROWS * COLS] = flat.T.astype(BF)


def side_kernel(x_in, grad_in, left, right, x, grad, sems):
    copies = [
        pltpu.make_async_copy(x_in, x, sems.at[0]),
        pltpu.make_async_copy(grad_in, grad, sems.at[1]),
    ]
    for copy in copies:
        copy.start()
    copies[0].wait()

    def x_member(m, carry):
        for r in range(ROWS):
            row = x[m, r].astype(F32)
            left[m, r] = row[0:8].astype(BF)
            right[m, r] = row[8:16].astype(BF)
        return carry

    lax.fori_loop(0, M, x_member, 0)
    copies[1].wait()

    def g_member(m, carry):
        for q in range(ROWS // 2):
            one = grad[m, 2 * q].astype(F32)
            two = grad[m, 2 * q + 1].astype(F32)
            left[m, ROWS + q] = jnp.concatenate([one[0:4], two[0:4]], axis=0).astype(BF)
            right[m, ROWS + q] = jnp.concatenate([one[12:16], two[12:16]], axis=0).astype(BF)
        return carry

    lax.fori_loop(0, M, g_member, 0)


def rim_rows(x, grad, left_x, right_x, left_g, right_g, at, out):
    def member(m, carry):
        for r in range(2):
            row = x[m, r].astype(F32)
            out[m, 4 * r] = left_x[m, r]
            out[m, 4 * r + 1] = row[0:8].astype(BF)
            out[m, 4 * r + 2] = row[8:16].astype(BF)
            out[m, 4 * r + 3] = right_x[m, r]
        before = left_g[m, 0].astype(F32)[at : at + 4]
        after = right_g[m, 0].astype(F32)[at : at + 4]
        line = jnp.concatenate([before, grad[m, 0].astype(F32), after], axis=0).astype(BF)
        for t in range(3):
            out[m, 8 + t] = line[8 * t : 8 * t + 8]
        return carry

    lax.fori_loop(0, M, member, 0)


def rim_kernel(*refs):
    rim_rows(*refs[0:6], 4, refs[13])
    rim_rows(*refs[6:12], 0, refs[14])


def adjoint_rows(far, grads, back):
    def member(m, carry):
        for p in range(ROWS // 2):
            spread = jnp.dot(
                far[p].reshape(K * 32, 128),
                grads[m, 2 * MID * p : 2 * MID * p + 128],
                preferred_element_type=F32,
            )
            start = pl.multiple_of(m * ROWS * COLS + 32 * p, 32)
            for k in range(K):
                back[pl.ds(start, 32), k * C : (k + 1) * C] = spread[32 * k : 32 * k + 32].astype(BF)
        return carry

    lax.fori_loop(0, M, member, 0)


def full_row(left, middle, right):
    return jnp.concatenate(
        [left.astype(F32), middle.astype(F32), right.astype(F32)], axis=0
    ).astype(BF)


def grad_row(left, out_grad, right, m, r):
    at = 4 * (r % 2)
    before = left[m, ROWS + r // 2].astype(F32)[at : at + 4]
    after = right[m, ROWS + r // 2].astype(F32)[at : at + 4]
    return jnp.concatenate([before, out_grad[m, r].astype(F32), after], axis=0)


def spread_pair(near, window, features, start):
    spread = jnp.dot(
        near.reshape(K * 2 * MID, 128), window, preferred_element_type=F32
    )
    for k in range(K):
        features[pl.ds(start, 2 * MID), k * C : (k + 1) * C] = spread[
            2 * MID * k : 2 * MID * k + 2 * MID
        ].astype(BF)


def activate(v, cotangent):
    slope = math.sqrt(2.0 / math.pi)
    square = v * v
    t = jnp.tanh(slope * v * (1.0 + 0.044715 * square))
    half = 0.5 * (1.0 + t)
    rise = half + 0.5 * v * (1.0 - t * t) * (slope * (1.0 + 3 * 0.044715 * square))
    return v * half, (cotangent * rise).astype(BF)


def inner_kernel(
    x, out_grad, near, left, right, weight_in, after,
    middle, result_out,
    wide, cotangent, features, mixed, result, weight, sems,
):
    copy = pltpu.make_async_copy(weight_in, weight, sems.at[0])
    copy.start()
    pairs = G_ROWS // 2 - 2

    def gather(m, carry):
        for r in range(ROWS):
            wide[m, WIDE * r : WIDE * r + WIDE] = full_row(left[m, r], x[m, r], right[m, r])
        for r in range(1, ROWS - 1):
            cotangent[m, MID * (r - 1) : MID * r] = grad_row(left, out_grad, right, m, r)
        for q in range(pairs):
            start = pl.multiple_of(m * pairs * 2 * MID + 2 * MID * q, 16)
            spread_pair(near[q + 1], wide[m, 2 * WIDE * q : 2 * WIDE * q + 128], features, start)
        return carry

    lax.fori_loop(0, M, gather, 0)
    copy.wait()
    mixed[...] = jnp.dot(features[...], weight[...], preferred_element_type=F32).reshape(
        mixed.shape
    )

    def finish(m, carry):
        for q in range(pairs):
            rows = slice(2 * MID * q, 2 * MID * q + 2 * MID)
            act, grad = activate(mixed[m, rows], cotangent[m, rows])
            middle[m, rows] = grad
            for part in range(2):
                own = act[MID * part + H : MID * part + H + COLS]
                r = 2 * q + part
                result[m, r] = (x[m, r + 1].astype(F32) + own).astype(BF)
        return carry

    lax.fori_loop(0, M, finish, 0)
    copy = pltpu.make_async_copy(result, result_out.at[:, 1 : ROWS - 1], sems.at[1])
    copy.start()
    copy.wait()


def outer_kernel(
    scale, core, x, x_turned, out_grad, near, far, top, bottom, left, right, middle, weight_in,
    tie, mine, other, grads_out, result_out,
    wide, cotangent, features, mixed, result, grads, back, weight, sems,
):
    copy = pltpu.make_async_copy(weight_in, weight, sems.at[0])
    copy.start()
    last = G_ROWS // 2 - 1

    def gather(m, carry):
        for r in range(2):
            for at, rim in ((r, top), (6 + r, bottom)):
                row = jnp.concatenate([rim[m, 4 * r + t].astype(F32) for t in range(4)], axis=0)
                wide[m, WIDE * at : WIDE * at + WIDE] = row.astype(BF)
            for at, own in ((2 + r, r), (4 + r, ROWS - 2 + r)):
                wide[m, WIDE * at : WIDE * at + WIDE] = full_row(
                    left[m, own], x[m, own], right[m, own]
                )
        for at, rim in ((0, top), (3, bottom)):
            cotangent[m, MID * at : MID * at + MID] = jnp.concatenate(
                [rim[m, 8 + t].astype(F32) for t in range(3)], axis=0
            )
        for at, own in ((1, 0), (2, ROWS - 1)):
            cotangent[m, MID * at : MID * at + MID] = grad_row(left, out_grad, right, m, own)
        for q, p in enumerate((0, last)):
            start = pl.multiple_of(m * 4 * MID + 2 * MID * q, 16)
            spread_pair(near[p], wide[m, 128 * q : 128 * q + 128], features, start)
        return carry

    lax.fori_loop(0, M, gather, 0)
    copy.wait()
    mixed[...] = jnp.dot(features[...], weight[...], preferred_element_type=F32).reshape(
        mixed.shape
    )

    def finish(m, carry):
        for q, p in enumerate((0, last)):
            rows = slice(2 * MID * q, 2 * MID * q + 2 * MID)
            act, grad = activate(mixed[m, rows], cotangent[m, rows])
            grads[m, 2 * MID * p : 2 * MID * p + 2 * MID] = grad
            part = 1 - q
            own = act[MID * part + H : MID * part + H + COLS]
            result[q, m] = (x[m, (ROWS - 1) * q].astype(F32) + own).astype(BF)
        grads[m, 2 * MID : 2 * MID * last] = middle[m]
        grads[m, G_ROWS * MID : G_PAD] = jnp.zeros((G_PAD - G_ROWS * MID, C), BF)
        return carry

    lax.fori_loop(0, M, finish, 0)
    copies = [
        pltpu.make_async_copy(grads, grads_out, sems.at[1]),
        pltpu.make_async_copy(result.at[0], result_out.at[:, 0], sems.at[2]),
        pltpu.make_async_copy(result.at[1], result_out.at[:, ROWS - 1], sems.at[3]),
    ]
    for copy in copies:
        copy.start()
    adjoint_rows(far, grads, back)
    first = core[0] == 0
    for k in range(K):
        part = scale * jnp.dot(
            x_turned[...], back[:, k * C : (k + 1) * C], preferred_element_type=F32
        )
        low = part[:, 0:128]
        high = part[:, 128:256]
        mine[:, 128 * k : 128 * k + 128] = jnp.where(first, low, high).astype(BF)
        other[:, 128 * k : 128 * k + 128] = jnp.where(first, high, low).astype(BF)
    for copy in copies:
        copy.wait()


def tail_kernel(grads_in, out_grad, far, weight_in, tie, in_grad, tied, back, weight, grads, sems):
    copy = pltpu.make_async_copy(weight_in, weight, sems.at[0])
    fetch = pltpu.make_async_copy(grads_in, grads, sems.at[1])
    fetch.start()
    copy.start()
    fetch.wait()
    adjoint_rows(far, grads, back)
    copy.wait()
    total = out_grad[...].reshape(M * ROWS * COLS, C).astype(F32)
    for k in range(K):
        total = total + lax.dot_general(
            back[:, k * C : (k + 1) * C],
            weight[k * C : (k + 1) * C],
            (((1,), (1,)), ((), ())),
            preferred_element_type=F32,
        )
    in_grad[...] = total.reshape(M, ROWS, COLS, C).astype(BF)


VM = pl.BlockSpec(memory_space=pltpu.VMEM)
SM = pl.BlockSpec(memory_space=pltpu.SMEM)
KEPT = pl.BlockSpec(memory_space=pl.ANY)
FAR = pl.BlockSpec(memory_space=pltpu.HBM)


def call(
    kernel, ins, outs, args, name,
    scratch=(), mib=8, flops=0, moved=1 << 20, tie=None, sems=0, away=(),
):
    aliases = {}
    out_specs = [VM] * len(outs)
    outs = [jax.ShapeDtypeStruct(*o) for o in outs]
    for shape, dtype in away:
        out_specs = out_specs + [FAR]
        outs = outs + [pltpu.HBM(shape, dtype)]
    if tie is not None:
        aliases = {len(args): len(outs)}
        ins = ins + [KEPT]
        args = args + (tie,)
        out_specs = out_specs + [KEPT]
        outs = outs + [jax.ShapeDtypeStruct(tie.shape, tie.dtype)]
    return pl.pallas_call(
        kernel,
        out_shape=outs,
        in_specs=ins,
        out_specs=out_specs,
        scratch_shapes=[pltpu.VMEM(*s) for s in scratch]
        + [pltpu.SemaphoreType.DMA((sems,))] * (sems > 0),
        input_output_aliases=aliases,
        cost_estimate=pl.CostEstimate(flops=flops, bytes_accessed=moved, transcendentals=0),
        compiler_params=pltpu.CompilerParams(vmem_limit_bytes=mib << 20),
        name=name,
    )(*args)


def edge(rows, block, width):
    return pl.BlockSpec((M, rows, width, C), lambda i: (0, block, 0, 0))


def send_sides(x, out_grad):
    shape = (M, ROWS + ROWS // 2, 8, C)
    to_left, to_right = call(
        side_kernel,
        [FAR] * 2,
        [(shape, BF)] * 2,
        (x, out_grad),
        "side",
        scratch=[(x.shape, BF)] * 2,
        mib=60,
        sems=2,
    )
    count = lax.axis_size("lon")
    left = lax.ppermute(to_right, "lon", [(i, (i + 1) % count) for i in range(count)])
    right = lax.ppermute(to_left, "lon", [((i + 1) % count, i) for i in range(count)])
    return left, right


def send_rims(x, out_grad, left, right, after):
    shape = (M, 11, 8, C)
    whole = pl.BlockSpec(shape, lambda i: (0, 0, 0, 0))
    ins = []
    for x_at, g_at in ((ROWS // 2 - 1, ROWS - 1), (0, 0)):
        ins += [edge(2, x_at, COLS), edge(1, g_at, COLS)]
        ins += [edge(2, x_at, 8)] * 2 + [edge(1, ROWS + g_at // 2, 8)] * 2
    up, down = pl.pallas_call(
        rim_kernel,
        grid=(1,),
        out_shape=[jax.ShapeDtypeStruct(shape, BF)] * 2,
        in_specs=ins + [KEPT],
        out_specs=[whole] * 2,
        cost_estimate=pl.CostEstimate(flops=0, bytes_accessed=1 << 18, transcendentals=0),
        compiler_params=pltpu.CompilerParams(vmem_limit_bytes=6 << 20),
        name="rim",
    )(*((x, out_grad, left, right, left, right) * 2), after)
    count = lax.axis_size("lat")
    top = lax.ppermute(up, "lat", [(i, i + 1) for i in range(count - 1)])
    bottom = lax.ppermute(down, "lat", [(i + 1, i) for i in range(count - 1)])
    return up, top, bottom


def reduce_gradient(mine, other, behind):
    half = K * C // CORES
    rows = C // YS
    share_rows = rows // ZS
    y_index = (lax.axis_index("lon") // ZS).reshape(1)
    got = lax.ppermute(other, "lat", core_swap())
    own, *sent = call(
        fold_kernel,
        [SM, VM, VM],
        [((rows, half), F32)] + [((rows, half), BF)] * 3,
        (y_index, mine, got),
        "fold",
    )
    parts = [lax.ppermute(sent[step - 1], "lon", y_shift(step)) for step in range(1, YS)]
    extra, own = behind(own)
    (joined,) = call(
        join_kernel, [VM] * 4, [((ZS, share_rows, half), BF)], (own, *parts), "join"
    )
    groups = [[y * ZS + z for z in range(ZS)] for y in range(YS)]
    shares = lax.all_to_all(joined, "lon", 0, 0, axis_index_groups=groups, tiled=True)
    (share,) = call(
        share_kernel, [VM], [((XS * CORES, share_rows, half), BF)], (shares,), "share"
    )
    shares = lax.all_to_all(share, ("ens", "lat"), 0, 0, tiled=True)
    (weight_grad,) = call(place_kernel, [VM], [((K, share_rows, C), F32)], (shares,), "place")
    return weight_grad, extra


def shards(members_in, out_grad, weight, basis_blocks, cycle_block, half_width):
    lat = lax.axis_index("lat")
    left, right = send_sides(members_in, out_grad)
    blocks = basis_blocks.shape[0]
    basis = jnp.pad(basis_blocks, ((0, 0), (0, 0), (0, 0), (0, 32 - TAPS))).reshape(blocks, K, 96)
    flipped = jnp.pad(
        basis_blocks[:, :, ::-1, ::-1], ((0, 0), (0, 0), (0, 0), (0, MID - TAPS))
    ).reshape(blocks, K, 72)
    gap = jnp.zeros((blocks, K, 32), F32)
    basis = jnp.concatenate([basis, gap, flipped, gap, gap[:, :, :24]], axis=2)

    near, far, x_turned = call(
        table_kernel,
        [SM] * 3 + [VM] * 2,
        [
            ((G_ROWS // 2, K, 2 * MID, 128), BF),
            ((ROWS // 2, K, 32, 128), BF),
            ((C, M * ROWS * COLS), BF),
        ],
        (cycle_block, half_width.T, (lat * ROWS).reshape(1), basis, members_in),
        "table",
        flops=1 << 24,
        moved=3 << 20,
    )
    up, top, bottom = send_rims(members_in, out_grad, left, right, far)
    flat_weight = pltpu.with_memory_space_constraint(weight.reshape(K * C, C), pltpu.HBM)
    cell_count = (
        M * lax.axis_size("ens") * ROWS * lax.axis_size("lat") * COLS * lax.axis_size("lon")
    )
    half_shape = (C, K * C // CORES)
    inner = (G_ROWS - 4) * MID
    middle, result = call(
        inner_kernel,
        [VM] * 5 + [FAR, KEPT],
        [((M, inner, C), BF)],
        (members_in, out_grad, near, left, right, flat_weight, up),
        "inner",
        scratch=[
            ((M, ROWS * WIDE, C), BF),
            ((M, inner, C), F32),
            ((M * inner, K * C), BF),
            ((M, inner, C), F32),
            ((M, ROWS - 2, COLS, C), BF),
            (flat_weight.shape, BF),
        ],
        mib=18,
        sems=2,
        flops=3 << 30,
        moved=4 << 20,
        away=[(members_in.shape, BF)],
    )
    outer = 4 * MID
    mine, other, grads, result = call(
        functools.partial(outer_kernel, 1.0 / math.sqrt(cell_count)),
        [SM] + [VM] * 10 + [FAR],
        [(half_shape, BF)] * 2,
        (
            lax.rem(lat, CORES).reshape(1),
            members_in,
            x_turned,
            out_grad,
            near,
            far,
            top,
            bottom,
            left,
            right,
            middle,
            flat_weight,
        ),
        "outer",
        scratch=[
            ((M, 8 * WIDE, C), BF),
            ((M, outer, C), F32),
            ((M * outer, K * C), BF),
            ((M, outer, C), F32),
            ((2, M, COLS, C), BF),
            ((M, G_PAD, C), BF),
            ((M * ROWS * COLS, K * C), BF),
            (flat_weight.shape, BF),
        ],
        mib=18,
        sems=4,
        flops=4 << 30,
        moved=4 << 20,
        away=[((M, G_PAD, C), BF)],
        tie=result,
    )

    def tail(tie):
        return call(
            tail_kernel,
            [FAR] + [VM] * 2 + [FAR],
            [(members_in.shape, BF)],
            (grads, out_grad, far, flat_weight),
            "tail",
            scratch=[
                ((M * ROWS * COLS, K * C), BF),
                (flat_weight.shape, BF),
                (grads.shape, BF),
            ],
            sems=2,
            mib=8,
            flops=2 << 30,
            moved=4 << 20,
            tie=tie,
        )

    weight_grad, in_grad = reduce_gradient(mine, other, tail)
    return (result, in_grad, weight_grad)


def solution(mesh):
    return jax.shard_map(
        shards,
        mesh=mesh,
        in_specs=(P("ens", "lat", "lon", None), P("ens", "lat", "lon", None), P(), P(), P(), P()),
        out_specs=(
            P("ens", "lat", "lon", None),
            P("ens", "lat", "lon", None),
            P(None, "lon", None),
        ),
        check_vma=False,
    )
```

```python
import functools
import math

import jax
import jax.numpy as jnp
from jax import lax
from jax.experimental import pallas as pl
from jax.experimental.pallas import tpu as pltpu
from jax.sharding import PartitionSpec as P

C = 256
K = 9
R = 1
H = 4
TAPS = 2 * H + 1

CORES = 2
YS = 4
ZS = 8
XS = 4

M = 4
ROWS = 8
COLS = 16
WIDE = COLS + 4 * H
MID = COLS + 2 * H
X_ROWS = ROWS + 4 * R
G_ROWS = ROWS + 2 * R
G_PAD = G_ROWS * MID + 32
BF = jnp.bfloat16
F32 = jnp.float32


def core_swap():
    return [(i, i ^ 1) for i in range(4)]


def y_swap(step):
    return [(y * ZS + z, (y ^ step) * ZS + z) for y in range(YS) for z in range(ZS)]


def fold_kernel(y, mine, got, own, *sent):
    rows = C // YS
    for step in range(YS):
        at = pl.multiple_of((y[0] ^ step) * rows, rows)
        total = mine[pl.ds(at, rows), :].astype(F32) + got[pl.ds(at, rows), :].astype(F32)
        if step == 0:
            own[...] = total
        else:
            sent[step - 1][...] = total.astype(BF)


def join_kernel(own, one, two, three, out):
    total = own[...] + one[...].astype(F32) + two[...].astype(F32) + three[...].astype(F32)
    out[...] = total.reshape(out.shape).astype(BF)


def share_kernel(shares, out):
    total = shares[0].astype(F32)
    for z in range(1, ZS):
        total = total + shares[z].astype(F32)
    for copy in range(XS * CORES):
        out[copy] = total.astype(BF)


def place_kernel(shares, out):
    half = C // CORES
    for core in range(CORES):
        total = shares[core].astype(F32)
        for x in range(1, XS):
            total = total + shares[x * CORES + core].astype(F32)
        for k in range(K):
            out[k, :, core * half : (core + 1) * half] = total[:, k * half : (k + 1) * half]


def table_kernel(cycles, widths, first, basis, x, near, far, x_turned):
    lane = lax.broadcasted_iota(jnp.int32, (1, 128), 1)
    total = cycles.shape[0]
    blocks = []
    reach = []
    for row in range(G_ROWS):
        cycle = jnp.clip(first[0] + (row - R), 0, total - 1)
        blocks.append(cycles[cycle])
        reach.append([widths[r, cycle] for r in range(3)])
    for p in range(G_ROWS // 2):
        bases = []
        for row in (2 * p, 2 * p + 1):
            limit = jnp.where(
                lane < 32, reach[row][0], jnp.where(lane < 64, reach[row][1], reach[row][2])
            )
            inside = jnp.abs((lane & 31) - H) <= limit
            base = jnp.where(inside, basis[blocks[row], :, 0:128], 0.0)
            bases.append(pltpu.roll(base, 32, 1) if row % 2 else base)
        for k in range(K):
            bands = [
                pltpu.roll(
                    jnp.broadcast_to(base[k : k + 1], (MID, 128)), 0, 1, stride=1, stride_axis=0
                )
                for base in bases
            ]
            near[p, k] = jnp.concatenate(bands, axis=0).astype(BF)
    for row in range(ROWS):
        base = jnp.zeros((K, 128), F32)
        for t in range(3):
            place = lane - MID * t
            inside = (place >= 0) & (place < TAPS) & (jnp.abs(place - H) <= reach[row + t][2 - t])
            base = base + jnp.where(inside, basis[blocks[row + t], :, 128:256], 0.0)
        if row % 2:
            base = pltpu.roll(base, MID, 1)
        for k in range(K):
            band = pltpu.roll(
                jnp.broadcast_to(base[k : k + 1], (COLS, 128)), 0, 1, stride=1, stride_axis=0
            )
            far[row // 2, k, COLS * (row % 2) : COLS * (row % 2) + COLS] = band.astype(BF)
    for m in range(M):
        flat = x[m].reshape(ROWS * COLS, C).astype(F32)
        x_turned[:, m * ROWS * COLS : (m + 1) * ROWS * COLS] = flat.T.astype(BF)


def side_kernel(x_in, grad_in, left, right, x, grad, sems):
    copies = [
        pltpu.make_async_copy(x_in, x, sems.at[0]),
        pltpu.make_async_copy(grad_in, grad, sems.at[1]),
    ]
    for copy in copies:
        copy.start()
    copies[0].wait()

    def x_member(m, carry):
        for r in range(ROWS):
            row = x[m, r].astype(F32)
            left[m, r] = row[0:8].astype(BF)
            right[m, r] = row[8:16].astype(BF)
        return carry

    lax.fori_loop(0, M, x_member, 0)
    copies[1].wait()

    def g_member(m, carry):
        for q in range(ROWS // 2):
            one = grad[m, 2 * q].astype(F32)
            two = grad[m, 2 * q + 1].astype(F32)
            left[m, ROWS + q] = jnp.concatenate([one[0:4], two[0:4]], axis=0).astype(BF)
            right[m, ROWS + q] = jnp.concatenate([one[12:16], two[12:16]], axis=0).astype(BF)
        return carry

    lax.fori_loop(0, M, g_member, 0)


def rim_rows(x, grad, left_x, right_x, left_g, right_g, at, out):
    def member(m, carry):
        for r in range(2):
            row = x[m, r].astype(F32)
            out[m, 4 * r] = left_x[m, r]
            out[m, 4 * r + 1] = row[0:8].astype(BF)
            out[m, 4 * r + 2] = row[8:16].astype(BF)
            out[m, 4 * r + 3] = right_x[m, r]
        before = left_g[m, 0].astype(F32)[at : at + 4]
        after = right_g[m, 0].astype(F32)[at : at + 4]
        line = jnp.concatenate([before, grad[m, 0].astype(F32), after], axis=0).astype(BF)
        for t in range(3):
            out[m, 8 + t] = line[8 * t : 8 * t + 8]
        return carry

    lax.fori_loop(0, M, member, 0)


def rim_kernel(*refs):
    rim_rows(*refs[0:6], 4, refs[13])
    rim_rows(*refs[6:12], 0, refs[14])


def adjoint_rows(far, grads, back):
    def member(m, carry):
        for p in range(ROWS // 2):
            spread = jnp.dot(
                far[p].reshape(K * 32, 128),
                grads[m, 2 * MID * p : 2 * MID * p + 128],
                preferred_element_type=F32,
            )
            start = pl.multiple_of(m * ROWS * COLS + 32 * p, 32)
            for k in range(K):
                back[pl.ds(start, 32), k * C : (k + 1) * C] = spread[32 * k : 32 * k + 32].astype(BF)
        return carry

    lax.fori_loop(0, M, member, 0)


def full_row(left, middle, right):
    return jnp.concatenate(
        [left.astype(F32), middle.astype(F32), right.astype(F32)], axis=0
    ).astype(BF)


def grad_row(left, out_grad, right, m, r):
    at = 4 * (r % 2)
    before = left[m, ROWS + r // 2].astype(F32)[at : at + 4]
    after = right[m, ROWS + r // 2].astype(F32)[at : at + 4]
    return jnp.concatenate([before, out_grad[m, r].astype(F32), after], axis=0)


def spread_pair(near, window, features, start):
    spread = jnp.dot(
        near.reshape(K * 2 * MID, 128), window, preferred_element_type=F32
    )
    for k in range(K):
        features[pl.ds(start, 2 * MID), k * C : (k + 1) * C] = spread[
            2 * MID * k : 2 * MID * k + 2 * MID
        ].astype(BF)


def activate(v, cotangent):
    slope = math.sqrt(2.0 / math.pi)
    square = v * v
    t = jnp.tanh(slope * v * (1.0 + 0.044715 * square))
    half = 0.5 * (1.0 + t)
    rise = half + 0.5 * v * (1.0 - t * t) * (slope * (1.0 + 3 * 0.044715 * square))
    return v * half, (cotangent * rise).astype(BF)


def inner_kernel(
    x, out_grad, near, left, right, weight_in, after,
    middle, result_out,
    wide, cotangent, features, mixed, result, weight, sems,
):
    copy = pltpu.make_async_copy(weight_in, weight, sems.at[0])
    copy.start()
    pairs = G_ROWS // 2 - 2

    def gather(m, carry):
        for r in range(ROWS):
            wide[m, WIDE * r : WIDE * r + WIDE] = full_row(left[m, r], x[m, r], right[m, r])
        for r in range(1, ROWS - 1):
            cotangent[m, MID * (r - 1) : MID * r] = grad_row(left, out_grad, right, m, r)
        for q in range(pairs):
            start = pl.multiple_of(m * pairs * 2 * MID + 2 * MID * q, 16)
            spread_pair(near[q + 1], wide[m, 2 * WIDE * q : 2 * WIDE * q + 128], features, start)
        return carry

    lax.fori_loop(0, M, gather, 0)
    copy.wait()
    mixed[...] = jnp.dot(features[...], weight[...], preferred_element_type=F32).reshape(
        mixed.shape
    )

    def finish(m, carry):
        for q in range(pairs):
            rows = slice(2 * MID * q, 2 * MID * q + 2 * MID)
            act, grad = activate(mixed[m, rows], cotangent[m, rows])
            middle[m, rows] = grad
            for part in range(2):
                own = act[MID * part + H : MID * part + H + COLS]
                r = 2 * q + part
                result[m, r] = (x[m, r + 1].astype(F32) + own).astype(BF)
        return carry

    lax.fori_loop(0, M, finish, 0)
    copy = pltpu.make_async_copy(result, result_out.at[:, 1 : ROWS - 1], sems.at[1])
    copy.start()
    copy.wait()


def outer_kernel(
    scale, core, x, x_turned, out_grad, near, far, top, bottom, left, right, middle, weight_in,
    tie, mine, other, grads_out, result_out,
    wide, cotangent, features, mixed, result, grads, back, weight, sems,
):
    copy = pltpu.make_async_copy(weight_in, weight, sems.at[0])
    copy.start()
    last = G_ROWS // 2 - 1

    def gather(m, carry):
        for r in range(2):
            for at, rim in ((r, top), (6 + r, bottom)):
                row = jnp.concatenate([rim[m, 4 * r + t].astype(F32) for t in range(4)], axis=0)
                wide[m, WIDE * at : WIDE * at + WIDE] = row.astype(BF)
            for at, own in ((2 + r, r), (4 + r, ROWS - 2 + r)):
                wide[m, WIDE * at : WIDE * at + WIDE] = full_row(
                    left[m, own], x[m, own], right[m, own]
                )
        for at, rim in ((0, top), (3, bottom)):
            cotangent[m, MID * at : MID * at + MID] = jnp.concatenate(
                [rim[m, 8 + t].astype(F32) for t in range(3)], axis=0
            )
        for at, own in ((1, 0), (2, ROWS - 1)):
            cotangent[m, MID * at : MID * at + MID] = grad_row(left, out_grad, right, m, own)
        for q, p in enumerate((0, last)):
            start = pl.multiple_of(m * 4 * MID + 2 * MID * q, 16)
            spread_pair(near[p], wide[m, 128 * q : 128 * q + 128], features, start)
        return carry

    lax.fori_loop(0, M, gather, 0)
    copy.wait()
    mixed[...] = jnp.dot(features[...], weight[...], preferred_element_type=F32).reshape(
        mixed.shape
    )

    def finish(m, carry):
        for q, p in enumerate((0, last)):
            rows = slice(2 * MID * q, 2 * MID * q + 2 * MID)
            act, grad = activate(mixed[m, rows], cotangent[m, rows])
            grads[m, 2 * MID * p : 2 * MID * p + 2 * MID] = grad
            part = 1 - q
            own = act[MID * part + H : MID * part + H + COLS]
            result[q, m] = (x[m, (ROWS - 1) * q].astype(F32) + own).astype(BF)
        grads[m, 2 * MID : 2 * MID * last] = middle[m]
        grads[m, G_ROWS * MID : G_PAD] = jnp.zeros((G_PAD - G_ROWS * MID, C), BF)
        return carry

    lax.fori_loop(0, M, finish, 0)
    copies = [
        pltpu.make_async_copy(grads, grads_out, sems.at[1]),
        pltpu.make_async_copy(result.at[0], result_out.at[:, 0], sems.at[2]),
        pltpu.make_async_copy(result.at[1], result_out.at[:, ROWS - 1], sems.at[3]),
    ]
    for copy in copies:
        copy.start()
    adjoint_rows(far, grads, back)
    first = core[0] == 0
    for k in range(K):
        part = scale * jnp.dot(
            x_turned[...], back[:, k * C : (k + 1) * C], preferred_element_type=F32
        )
        low = part[:, 0:128]
        high = part[:, 128:256]
        mine[:, 128 * k : 128 * k + 128] = jnp.where(first, low, high).astype(BF)
        other[:, 128 * k : 128 * k + 128] = jnp.where(first, high, low).astype(BF)
    for copy in copies:
        copy.wait()


def tail_kernel(grads_in, out_grad, far, weight_in, tie, in_grad, tied, back, weight, grads, sems):
    copy = pltpu.make_async_copy(weight_in, weight, sems.at[0])
    fetch = pltpu.make_async_copy(grads_in, grads, sems.at[1])
    fetch.start()
    copy.start()
    fetch.wait()
    adjoint_rows(far, grads, back)
    copy.wait()
    total = out_grad[...].reshape(M * ROWS * COLS, C).astype(F32)
    for k in range(K):
        total = total + lax.dot_general(
            back[:, k * C : (k + 1) * C],
            weight[k * C : (k + 1) * C],
            (((1,), (1,)), ((), ())),
            preferred_element_type=F32,
        )
    in_grad[...] = total.reshape(M, ROWS, COLS, C).astype(BF)


VM = pl.BlockSpec(memory_space=pltpu.VMEM)
SM = pl.BlockSpec(memory_space=pltpu.SMEM)
KEPT = pl.BlockSpec(memory_space=pl.ANY)
FAR = pl.BlockSpec(memory_space=pltpu.HBM)


def call(
    kernel, ins, outs, args, name,
    scratch=(), mib=8, flops=0, moved=1 << 20, tie=None, sems=0, away=(),
):
    aliases = {}
    out_specs = [VM] * len(outs)
    outs = [jax.ShapeDtypeStruct(*o) for o in outs]
    for shape, dtype in away:
        out_specs = out_specs + [FAR]
        outs = outs + [pltpu.HBM(shape, dtype)]
    if tie is not None:
        aliases = {len(args): len(outs)}
        ins = ins + [KEPT]
        args = args + (tie,)
        out_specs = out_specs + [KEPT]
        outs = outs + [jax.ShapeDtypeStruct(tie.shape, tie.dtype)]
    return pl.pallas_call(
        kernel,
        out_shape=outs,
        in_specs=ins,
        out_specs=out_specs,
        scratch_shapes=[pltpu.VMEM(*s) for s in scratch]
        + [pltpu.SemaphoreType.DMA((sems,))] * (sems > 0),
        input_output_aliases=aliases,
        cost_estimate=pl.CostEstimate(flops=flops, bytes_accessed=moved, transcendentals=0),
        compiler_params=pltpu.CompilerParams(vmem_limit_bytes=mib << 20),
        name=name,
    )(*args)


def edge(rows, block, width):
    return pl.BlockSpec((M, rows, width, C), lambda i: (0, block, 0, 0))


def send_sides(x, out_grad):
    shape = (M, ROWS + ROWS // 2, 8, C)
    to_left, to_right = call(
        side_kernel,
        [FAR] * 2,
        [(shape, BF)] * 2,
        (
            pltpu.with_memory_space_constraint(x, pltpu.HBM),
            pltpu.with_memory_space_constraint(out_grad, pltpu.HBM),
        ),
        "side",
        scratch=[(x.shape, BF)] * 2,
        sems=2,
    )
    count = lax.axis_size("lon")
    left = lax.ppermute(to_right, "lon", [(i, (i + 1) % count) for i in range(count)])
    right = lax.ppermute(to_left, "lon", [((i + 1) % count, i) for i in range(count)])
    return left, right


def send_rims(x, out_grad, left, right, after):
    shape = (M, 11, 8, C)
    whole = pl.BlockSpec(shape, lambda i: (0, 0, 0, 0))
    ins = []
    for x_at, g_at in ((ROWS // 2 - 1, ROWS - 1), (0, 0)):
        ins += [edge(2, x_at, COLS), edge(1, g_at, COLS)]
        ins += [edge(2, x_at, 8)] * 2 + [edge(1, ROWS + g_at // 2, 8)] * 2
    up, down = pl.pallas_call(
        rim_kernel,
        grid=(1,),
        out_shape=[jax.ShapeDtypeStruct(shape, BF)] * 2,
        in_specs=ins + [KEPT],
        out_specs=[whole] * 2,
        cost_estimate=pl.CostEstimate(flops=0, bytes_accessed=1 << 18, transcendentals=0),
        compiler_params=pltpu.CompilerParams(vmem_limit_bytes=6 << 20),
        name="rim",
    )(*((x, out_grad, left, right, left, right) * 2), after)
    count = lax.axis_size("lat")
    top = lax.ppermute(up, "lat", [(i, i + 1) for i in range(count - 1)])
    bottom = lax.ppermute(down, "lat", [(i + 1, i) for i in range(count - 1)])
    return up, top, bottom


def reduce_gradient(mine, other, behind):
    half = K * C // CORES
    rows = C // YS
    share_rows = rows // ZS
    y_index = (lax.axis_index("lon") // ZS).reshape(1)
    got = lax.ppermute(other, "lat", core_swap())
    own, *sent = call(
        fold_kernel,
        [SM, VM, VM],
        [((rows, half), F32)] + [((rows, half), BF)] * 3,
        (y_index, mine, got),
        "fold",
    )
    parts = [lax.ppermute(sent[step - 1], "lon", y_swap(step)) for step in (2, 1, 3)]
    extra, own = behind(own)
    (joined,) = call(
        join_kernel, [VM] * 4, [((ZS, share_rows, half), BF)], (own, *parts), "join"
    )
    groups = [[y * ZS + z for z in range(ZS)] for y in range(YS)]
    shares = lax.all_to_all(joined, "lon", 0, 0, axis_index_groups=groups, tiled=True)
    (share,) = call(
        share_kernel, [VM], [((XS * CORES, share_rows, half), BF)], (shares,), "share"
    )
    shares = lax.all_to_all(share, ("ens", "lat"), 0, 0, tiled=True)
    (weight_grad,) = call(place_kernel, [VM], [((K, share_rows, C), F32)], (shares,), "place")
    return weight_grad, extra


def shards(members_in, out_grad, weight, basis_blocks, cycle_block, half_width):
    lat = lax.axis_index("lat")
    left, right = send_sides(members_in, out_grad)
    blocks = basis_blocks.shape[0]
    basis = jnp.pad(basis_blocks, ((0, 0), (0, 0), (0, 0), (0, 32 - TAPS))).reshape(blocks, K, 96)
    flipped = jnp.pad(
        basis_blocks[:, :, ::-1, ::-1], ((0, 0), (0, 0), (0, 0), (0, MID - TAPS))
    ).reshape(blocks, K, 72)
    gap = jnp.zeros((blocks, K, 32), F32)
    basis = jnp.concatenate([basis, gap, flipped, gap, gap[:, :, :24]], axis=2)

    near, far, x_turned = call(
        table_kernel,
        [SM] * 3 + [VM] * 2,
        [
            ((G_ROWS // 2, K, 2 * MID, 128), BF),
            ((ROWS // 2, K, 32, 128), BF),
            ((C, M * ROWS * COLS), BF),
        ],
        (cycle_block, half_width.T, (lat * ROWS).reshape(1), basis, members_in),
        "table",
        flops=1 << 24,
        moved=3 << 20,
    )
    up, top, bottom = send_rims(members_in, out_grad, left, right, far)
    flat_weight = pltpu.with_memory_space_constraint(weight.reshape(K * C, C), pltpu.HBM)
    cell_count = (
        M * lax.axis_size("ens") * ROWS * lax.axis_size("lat") * COLS * lax.axis_size("lon")
    )
    half_shape = (C, K * C // CORES)
    inner = (G_ROWS - 4) * MID
    middle, result = call(
        inner_kernel,
        [VM] * 5 + [FAR, KEPT],
        [((M, inner, C), BF)],
        (members_in, out_grad, near, left, right, flat_weight, up),
        "inner",
        scratch=[
            ((M, ROWS * WIDE, C), BF),
            ((M, inner, C), F32),
            ((M * inner, K * C), BF),
            ((M, inner, C), F32),
            ((M, ROWS - 2, COLS, C), BF),
            (flat_weight.shape, BF),
        ],
        mib=18,
        sems=2,
        flops=3 << 30,
        moved=4 << 20,
        away=[(members_in.shape, BF)],
    )
    outer = 4 * MID
    mine, other, grads, result = call(
        functools.partial(outer_kernel, 1.0 / math.sqrt(cell_count)),
        [SM] + [VM] * 10 + [FAR],
        [(half_shape, BF)] * 2,
        (
            lax.rem(lat, CORES).reshape(1),
            members_in,
            x_turned,
            out_grad,
            near,
            far,
            top,
            bottom,
            left,
            right,
            middle,
            flat_weight,
        ),
        "outer",
        scratch=[
            ((M, 8 * WIDE, C), BF),
            ((M, outer, C), F32),
            ((M * outer, K * C), BF),
            ((M, outer, C), F32),
            ((2, M, COLS, C), BF),
            ((M, G_PAD, C), BF),
            ((M * ROWS * COLS, K * C), BF),
            (flat_weight.shape, BF),
        ],
        mib=18,
        sems=4,
        flops=4 << 30,
        moved=4 << 20,
        away=[((M, G_PAD, C), BF)],
        tie=result,
    )

    def tail(tie):
        return call(
            tail_kernel,
            [FAR] + [VM] * 2 + [FAR],
            [(members_in.shape, BF)],
            (grads, out_grad, far, flat_weight),
            "tail",
            scratch=[
                ((M * ROWS * COLS, K * C), BF),
                (flat_weight.shape, BF),
                (grads.shape, BF),
            ],
            sems=2,
            mib=8,
            flops=2 << 30,
            moved=4 << 20,
            tie=tie,
        )

    weight_grad, in_grad = reduce_gradient(mine, other, tail)
    return (result, in_grad, weight_grad)


def solution(mesh):
    return jax.shard_map(
        shards,
        mesh=mesh,
        in_specs=(P("ens", "lat", "lon", None), P("ens", "lat", "lon", None), P(), P(), P(), P()),
        out_specs=(
            P("ens", "lat", "lon", None),
            P("ens", "lat", "lon", None),
            P(None, "lon", None),
        ),
        check_vma=False,
    )
```

```python
import functools
import math

import jax
import jax.numpy as jnp
from jax import lax
from jax.experimental import pallas as pl
from jax.experimental.pallas import tpu as pltpu
from jax.sharding import PartitionSpec as P

C = 256
K = 9
R = 1
H = 4
TAPS = 2 * H + 1

CORES = 2
YS = 4
ZS = 8
XS = 4

M = 4
ROWS = 8
COLS = 16
WIDE = COLS + 4 * H
MID = COLS + 2 * H
X_ROWS = ROWS + 4 * R
G_ROWS = ROWS + 2 * R
G_PAD = G_ROWS * MID + 32
BF = jnp.bfloat16
F32 = jnp.float32


def core_swap():
    return [(i, i ^ 1) for i in range(4)]


def y_swap(step):
    return [(y * ZS + z, (y ^ step) * ZS + z) for y in range(YS) for z in range(ZS)]


def fold_kernel(y, mine, got, own, *sent):
    rows = C // YS
    for step in range(YS):
        at = pl.multiple_of((y[0] ^ step) * rows, rows)
        total = mine[pl.ds(at, rows), :].astype(F32) + got[pl.ds(at, rows), :].astype(F32)
        if step == 0:
            own[...] = total
        else:
            sent[step - 1][...] = total.astype(BF)


def join_kernel(own, one, two, three, out):
    total = own[...] + one[...].astype(F32) + two[...].astype(F32) + three[...].astype(F32)
    out[...] = total.reshape(out.shape).astype(BF)


def share_kernel(shares, out):
    total = shares[0].astype(F32)
    for z in range(1, ZS):
        total = total + shares[z].astype(F32)
    for copy in range(XS * CORES):
        out[copy] = total.astype(BF)


def place_kernel(shares, out):
    half = C // CORES
    for core in range(CORES):
        total = shares[core].astype(F32)
        for x in range(1, XS):
            total = total + shares[x * CORES + core].astype(F32)
        for k in range(K):
            out[k, :, core * half : (core + 1) * half] = total[:, k * half : (k + 1) * half]


def table_kernel(cycles, widths, first, basis, x, near, far, x_turned):
    lane = lax.broadcasted_iota(jnp.int32, (1, 128), 1)
    total = cycles.shape[0]
    blocks = []
    reach = []
    for row in range(G_ROWS):
        cycle = jnp.clip(first[0] + (row - R), 0, total - 1)
        blocks.append(cycles[cycle])
        reach.append([widths[r, cycle] for r in range(3)])
    for p in range(G_ROWS // 2):
        bases = []
        for row in (2 * p, 2 * p + 1):
            limit = jnp.where(
                lane < 32, reach[row][0], jnp.where(lane < 64, reach[row][1], reach[row][2])
            )
            inside = jnp.abs((lane & 31) - H) <= limit
            base = jnp.where(inside, basis[blocks[row], :, 0:128], 0.0)
            bases.append(pltpu.roll(base, 32, 1) if row % 2 else base)
        for k in range(K):
            bands = [
                pltpu.roll(
                    jnp.broadcast_to(base[k : k + 1], (MID, 128)), 0, 1, stride=1, stride_axis=0
                )
                for base in bases
            ]
            near[p, k] = jnp.concatenate(bands, axis=0).astype(BF)
    for row in range(ROWS):
        base = jnp.zeros((K, 128), F32)
        for t in range(3):
            place = lane - MID * t
            inside = (place >= 0) & (place < TAPS) & (jnp.abs(place - H) <= reach[row + t][2 - t])
            base = base + jnp.where(inside, basis[blocks[row + t], :, 128:256], 0.0)
        if row % 2:
            base = pltpu.roll(base, MID, 1)
        for k in range(K):
            band = pltpu.roll(
                jnp.broadcast_to(base[k : k + 1], (COLS, 128)), 0, 1, stride=1, stride_axis=0
            )
            far[row // 2, k, COLS * (row % 2) : COLS * (row % 2) + COLS] = band.astype(BF)
    for m in range(M):
        flat = x[m].reshape(ROWS * COLS, C).astype(F32)
        x_turned[:, m * ROWS * COLS : (m + 1) * ROWS * COLS] = flat.T.astype(BF)


def side_kernel(x_in, grad_in, left, right, x, grad, sems):
    copies = [
        pltpu.make_async_copy(x_in, x, sems.at[0]),
        pltpu.make_async_copy(grad_in, grad, sems.at[1]),
    ]
    for copy in copies:
        copy.start()
    copies[0].wait()

    def x_member(m, carry):
        for r in range(ROWS):
            row = x[m, r].astype(F32)
            left[m, r] = row[0:8].astype(BF)
            right[m, r] = row[8:16].astype(BF)
        return carry

    lax.fori_loop(0, M, x_member, 0)
    copies[1].wait()

    def g_member(m, carry):
        for q in range(ROWS // 2):
            one = grad[m, 2 * q].astype(F32)
            two = grad[m, 2 * q + 1].astype(F32)
            left[m, ROWS + q] = jnp.concatenate([one[0:4], two[0:4]], axis=0).astype(BF)
            right[m, ROWS + q] = jnp.concatenate([one[12:16], two[12:16]], axis=0).astype(BF)
        return carry

    lax.fori_loop(0, M, g_member, 0)


def rim_rows(x, grad, left_x, right_x, left_g, right_g, at, out):
    def member(m, carry):
        for r in range(2):
            row = x[m, r].astype(F32)
            out[m, 4 * r] = left_x[m, r]
            out[m, 4 * r + 1] = row[0:8].astype(BF)
            out[m, 4 * r + 2] = row[8:16].astype(BF)
            out[m, 4 * r + 3] = right_x[m, r]
        before = left_g[m, 0].astype(F32)[at : at + 4]
        after = right_g[m, 0].astype(F32)[at : at + 4]
        line = jnp.concatenate([before, grad[m, 0].astype(F32), after], axis=0).astype(BF)
        for t in range(3):
            out[m, 8 + t] = line[8 * t : 8 * t + 8]
        return carry

    lax.fori_loop(0, M, member, 0)


def rim_kernel(*refs):
    even = refs[13][0] == 0
    pair, cross = refs[14], refs[15]

    @pl.when(even)
    def _():
        rim_rows(*refs[0:6], 4, pair)
        rim_rows(*refs[6:12], 0, cross)

    @pl.when(jnp.logical_not(even))
    def _():
        rim_rows(*refs[6:12], 0, pair)
        rim_rows(*refs[0:6], 4, cross)


def adjoint_rows(far, grads, back):
    def member(m, carry):
        for p in range(ROWS // 2):
            spread = jnp.dot(
                far[p].reshape(K * 32, 128),
                grads[m, 2 * MID * p : 2 * MID * p + 128],
                preferred_element_type=F32,
            )
            start = pl.multiple_of(m * ROWS * COLS + 32 * p, 32)
            for k in range(K):
                back[pl.ds(start, 32), k * C : (k + 1) * C] = spread[32 * k : 32 * k + 32].astype(BF)
        return carry

    lax.fori_loop(0, M, member, 0)


def full_row(left, middle, right):
    return jnp.concatenate(
        [left.astype(F32), middle.astype(F32), right.astype(F32)], axis=0
    ).astype(BF)


def grad_row(left, out_grad, right, m, r):
    at = 4 * (r % 2)
    before = left[m, ROWS + r // 2].astype(F32)[at : at + 4]
    after = right[m, ROWS + r // 2].astype(F32)[at : at + 4]
    return jnp.concatenate([before, out_grad[m, r].astype(F32), after], axis=0)


def spread_pair(near, window, features, start):
    spread = jnp.dot(
        near.reshape(K * 2 * MID, 128), window, preferred_element_type=F32
    )
    for k in range(K):
        features[pl.ds(start, 2 * MID), k * C : (k + 1) * C] = spread[
            2 * MID * k : 2 * MID * k + 2 * MID
        ].astype(BF)


def activate(v, cotangent):
    slope = math.sqrt(2.0 / math.pi)
    square = v * v
    t = jnp.tanh(slope * v * (1.0 + 0.044715 * square))
    half = 0.5 * (1.0 + t)
    rise = half + 0.5 * v * (1.0 - t * t) * (slope * (1.0 + 3 * 0.044715 * square))
    return v * half, (cotangent * rise).astype(BF)


def inner_kernel(
    x, out_grad, near, left, right, weight_in, after,
    middle, result_out,
    wide, cotangent, features, mixed, result, weight, sems,
):
    copy = pltpu.make_async_copy(weight_in, weight, sems.at[0])
    copy.start()
    pairs = G_ROWS // 2 - 2

    def gather(m, carry):
        for r in range(ROWS):
            wide[m, WIDE * r : WIDE * r + WIDE] = full_row(left[m, r], x[m, r], right[m, r])
        for r in range(1, ROWS - 1):
            cotangent[m, MID * (r - 1) : MID * r] = grad_row(left, out_grad, right, m, r)
        for q in range(pairs):
            start = pl.multiple_of(m * pairs * 2 * MID + 2 * MID * q, 16)
            spread_pair(near[q + 1], wide[m, 2 * WIDE * q : 2 * WIDE * q + 128], features, start)
        return carry

    lax.fori_loop(0, M, gather, 0)
    copy.wait()
    mixed[...] = jnp.dot(features[...], weight[...], preferred_element_type=F32).reshape(
        mixed.shape
    )

    def finish(m, carry):
        for q in range(pairs):
            rows = slice(2 * MID * q, 2 * MID * q + 2 * MID)
            act, grad = activate(mixed[m, rows], cotangent[m, rows])
            middle[m, rows] = grad
            for part in range(2):
                own = act[MID * part + H : MID * part + H + COLS]
                r = 2 * q + part
                result[m, r] = (x[m, r + 1].astype(F32) + own).astype(BF)
        return carry

    lax.fori_loop(0, M, finish, 0)
    copy = pltpu.make_async_copy(result, result_out.at[:, 1 : ROWS - 1], sems.at[1])
    copy.start()
    copy.wait()


def outer_kernel(
    scale, core, x, x_turned, out_grad, near, far, paired, crossed, left, right, middle, weight_in,
    tie, mine, other, grads_out, result_out,
    wide, cotangent, features, mixed, result, grads, back, weight, sems,
):
    copy = pltpu.make_async_copy(weight_in, weight, sems.at[0])
    copy.start()
    last = G_ROWS // 2 - 1

    def gather(top, bottom, m, carry):
        for r in range(2):
            for at, rim in ((r, top), (6 + r, bottom)):
                row = jnp.concatenate([rim[m, 4 * r + t].astype(F32) for t in range(4)], axis=0)
                wide[m, WIDE * at : WIDE * at + WIDE] = row.astype(BF)
            for at, own in ((2 + r, r), (4 + r, ROWS - 2 + r)):
                wide[m, WIDE * at : WIDE * at + WIDE] = full_row(
                    left[m, own], x[m, own], right[m, own]
                )
        for at, rim in ((0, top), (3, bottom)):
            cotangent[m, MID * at : MID * at + MID] = jnp.concatenate(
                [rim[m, 8 + t].astype(F32) for t in range(3)], axis=0
            )
        for at, own in ((1, 0), (2, ROWS - 1)):
            cotangent[m, MID * at : MID * at + MID] = grad_row(left, out_grad, right, m, own)
        for q, p in enumerate((0, last)):
            start = pl.multiple_of(m * 4 * MID + 2 * MID * q, 16)
            spread_pair(near[p], wide[m, 128 * q : 128 * q + 128], features, start)
        return carry

    first = core[0] == 0

    @pl.when(first)
    def _():
        lax.fori_loop(0, M, functools.partial(gather, crossed, paired), 0)

    @pl.when(jnp.logical_not(first))
    def _():
        lax.fori_loop(0, M, functools.partial(gather, paired, crossed), 0)

    copy.wait()
    mixed[...] = jnp.dot(features[...], weight[...], preferred_element_type=F32).reshape(
        mixed.shape
    )

    def finish(m, carry):
        for q, p in enumerate((0, last)):
            rows = slice(2 * MID * q, 2 * MID * q + 2 * MID)
            act, grad = activate(mixed[m, rows], cotangent[m, rows])
            grads[m, 2 * MID * p : 2 * MID * p + 2 * MID] = grad
            part = 1 - q
            own = act[MID * part + H : MID * part + H + COLS]
            result[q, m] = (x[m, (ROWS - 1) * q].astype(F32) + own).astype(BF)
        grads[m, 2 * MID : 2 * MID * last] = middle[m]
        grads[m, G_ROWS * MID : G_PAD] = jnp.zeros((G_PAD - G_ROWS * MID, C), BF)
        return carry

    lax.fori_loop(0, M, finish, 0)
    copies = [
        pltpu.make_async_copy(grads, grads_out, sems.at[1]),
        pltpu.make_async_copy(result.at[0], result_out.at[:, 0], sems.at[2]),
        pltpu.make_async_copy(result.at[1], result_out.at[:, ROWS - 1], sems.at[3]),
    ]
    for copy in copies:
        copy.start()
    adjoint_rows(far, grads, back)
    for k in range(K):
        part = scale * jnp.dot(
            x_turned[...], back[:, k * C : (k + 1) * C], preferred_element_type=F32
        )
        low = part[:, 0:128]
        high = part[:, 128:256]
        mine[:, 128 * k : 128 * k + 128] = jnp.where(first, low, high).astype(BF)
        other[:, 128 * k : 128 * k + 128] = jnp.where(first, high, low).astype(BF)
    for copy in copies:
        copy.wait()


def tail_kernel(grads_in, out_grad, far, weight_in, tie, in_grad, tied, back, weight, grads, sems):
    copy = pltpu.make_async_copy(weight_in, weight, sems.at[0])
    fetch = pltpu.make_async_copy(grads_in, grads, sems.at[1])
    fetch.start()
    copy.start()
    fetch.wait()
    adjoint_rows(far, grads, back)
    copy.wait()
    total = out_grad[...].reshape(M * ROWS * COLS, C).astype(F32)
    for k in range(K):
        total = total + lax.dot_general(
            back[:, k * C : (k + 1) * C],
            weight[k * C : (k + 1) * C],
            (((1,), (1,)), ((), ())),
            preferred_element_type=F32,
        )
    in_grad[...] = total.reshape(M, ROWS, COLS, C).astype(BF)


VM = pl.BlockSpec(memory_space=pltpu.VMEM)
SM = pl.BlockSpec(memory_space=pltpu.SMEM)
KEPT = pl.BlockSpec(memory_space=pl.ANY)
FAR = pl.BlockSpec(memory_space=pltpu.HBM)


def call(
    kernel, ins, outs, args, name,
    scratch=(), mib=8, flops=0, moved=1 << 20, tie=None, sems=0, away=(),
):
    aliases = {}
    out_specs = [VM] * len(outs)
    outs = [jax.ShapeDtypeStruct(*o) for o in outs]
    for shape, dtype in away:
        out_specs = out_specs + [FAR]
        outs = outs + [pltpu.HBM(shape, dtype)]
    if tie is not None:
        aliases = {len(args): len(outs)}
        ins = ins + [KEPT]
        args = args + (tie,)
        out_specs = out_specs + [KEPT]
        outs = outs + [jax.ShapeDtypeStruct(tie.shape, tie.dtype)]
    return pl.pallas_call(
        kernel,
        out_shape=outs,
        in_specs=ins,
        out_specs=out_specs,
        scratch_shapes=[pltpu.VMEM(*s) for s in scratch]
        + [pltpu.SemaphoreType.DMA((sems,))] * (sems > 0),
        input_output_aliases=aliases,
        cost_estimate=pl.CostEstimate(flops=flops, bytes_accessed=moved, transcendentals=0),
        compiler_params=pltpu.CompilerParams(vmem_limit_bytes=mib << 20),
        name=name,
    )(*args)


def edge(rows, block, width):
    return pl.BlockSpec((M, rows, width, C), lambda i: (0, block, 0, 0))


def send_sides(x, out_grad):
    shape = (M, ROWS + ROWS // 2, 8, C)
    to_left, to_right = call(
        side_kernel,
        [FAR] * 2,
        [(shape, BF)] * 2,
        (
            pltpu.with_memory_space_constraint(x, pltpu.HBM),
            pltpu.with_memory_space_constraint(out_grad, pltpu.HBM),
        ),
        "side",
        scratch=[(x.shape, BF)] * 2,
        sems=2,
    )
    count = lax.axis_size("lon")
    left = lax.ppermute(to_right, "lon", [(i, (i + 1) % count) for i in range(count)])
    right = lax.ppermute(to_left, "lon", [((i + 1) % count, i) for i in range(count)])
    return left, right


def send_rims(core, x, out_grad, left, right, after):
    shape = (M, 11, 8, C)
    whole = pl.BlockSpec(shape, lambda i: (0, 0, 0, 0))
    ins = []
    for x_at, g_at in ((ROWS // 2 - 1, ROWS - 1), (0, 0)):
        ins += [edge(2, x_at, COLS), edge(1, g_at, COLS)]
        ins += [edge(2, x_at, 8)] * 2 + [edge(1, ROWS + g_at // 2, 8)] * 2
    pair, cross = pl.pallas_call(
        rim_kernel,
        grid=(1,),
        out_shape=[jax.ShapeDtypeStruct(shape, BF)] * 2,
        in_specs=ins + [KEPT, SM],
        out_specs=[whole] * 2,
        cost_estimate=pl.CostEstimate(flops=0, bytes_accessed=1 << 18, transcendentals=0),
        compiler_params=pltpu.CompilerParams(vmem_limit_bytes=6 << 20),
        name="rim",
    )(*((x, out_grad, left, right, left, right) * 2), after, core)
    crossed = lax.ppermute(cross, "lat", [(1, 2), (2, 1)])
    paired = lax.ppermute(pair, "lat", core_swap())
    return pair, paired, crossed


def reduce_gradient(mine, other, behind):
    half = K * C // CORES
    rows = C // YS
    share_rows = rows // ZS
    y_index = (lax.axis_index("lon") // ZS).reshape(1)
    got = lax.ppermute(other, "lat", core_swap())
    own, *sent = call(
        fold_kernel,
        [SM, VM, VM],
        [((rows, half), F32)] + [((rows, half), BF)] * 3,
        (y_index, mine, got),
        "fold",
    )
    parts = [lax.ppermute(sent[step - 1], "lon", y_swap(step)) for step in (2, 1, 3)]
    extra, own = behind(own)
    (joined,) = call(
        join_kernel, [VM] * 4, [((ZS, share_rows, half), BF)], (own, *parts), "join"
    )
    groups = [[y * ZS + z for z in range(ZS)] for y in range(YS)]
    shares = lax.all_to_all(joined, "lon", 0, 0, axis_index_groups=groups, tiled=True)
    (share,) = call(
        share_kernel, [VM], [((XS * CORES, share_rows, half), BF)], (shares,), "share"
    )
    shares = lax.all_to_all(share, ("ens", "lat"), 0, 0, tiled=True)
    (weight_grad,) = call(place_kernel, [VM], [((K, share_rows, C), F32)], (shares,), "place")
    return weight_grad, extra


def shards(members_in, out_grad, weight, basis_blocks, cycle_block, half_width):
    lat = lax.axis_index("lat")
    left, right = send_sides(members_in, out_grad)
    blocks = basis_blocks.shape[0]
    basis = jnp.pad(basis_blocks, ((0, 0), (0, 0), (0, 0), (0, 32 - TAPS))).reshape(blocks, K, 96)
    flipped = jnp.pad(
        basis_blocks[:, :, ::-1, ::-1], ((0, 0), (0, 0), (0, 0), (0, MID - TAPS))
    ).reshape(blocks, K, 72)
    gap = jnp.zeros((blocks, K, 32), F32)
    basis = jnp.concatenate([basis, gap, flipped, gap, gap[:, :, :24]], axis=2)

    near, far, x_turned = call(
        table_kernel,
        [SM] * 3 + [VM] * 2,
        [
            ((G_ROWS // 2, K, 2 * MID, 128), BF),
            ((ROWS // 2, K, 32, 128), BF),
            ((C, M * ROWS * COLS), BF),
        ],
        (cycle_block, half_width.T, (lat * ROWS).reshape(1), basis, members_in),
        "table",
        flops=1 << 24,
        moved=3 << 20,
    )
    core = lax.rem(lat, CORES).reshape(1)
    pair, paired, crossed = send_rims(core, members_in, out_grad, left, right, far)
    flat_weight = pltpu.with_memory_space_constraint(weight.reshape(K * C, C), pltpu.HBM)
    cell_count = (
        M * lax.axis_size("ens") * ROWS * lax.axis_size("lat") * COLS * lax.axis_size("lon")
    )
    half_shape = (C, K * C // CORES)
    inner = (G_ROWS - 4) * MID
    middle, result = call(
        inner_kernel,
        [VM] * 5 + [FAR, KEPT],
        [((M, inner, C), BF)],
        (members_in, out_grad, near, left, right, flat_weight, pair),
        "inner",
        scratch=[
            ((M, ROWS * WIDE, C), BF),
            ((M, inner, C), F32),
            ((M * inner, K * C), BF),
            ((M, inner, C), F32),
            ((M, ROWS - 2, COLS, C), BF),
            (flat_weight.shape, BF),
        ],
        mib=18,
        sems=2,
        flops=3 << 30,
        moved=4 << 20,
        away=[(members_in.shape, BF)],
    )
    outer = 4 * MID
    mine, other, grads, result = call(
        functools.partial(outer_kernel, 1.0 / math.sqrt(cell_count)),
        [SM] + [VM] * 10 + [FAR],
        [(half_shape, BF)] * 2,
        (
            core,
            members_in,
            x_turned,
            out_grad,
            near,
            far,
            paired,
            crossed,
            left,
            right,
            middle,
            flat_weight,
        ),
        "outer",
        scratch=[
            ((M, 8 * WIDE, C), BF),
            ((M, outer, C), F32),
            ((M * outer, K * C), BF),
            ((M, outer, C), F32),
            ((2, M, COLS, C), BF),
            ((M, G_PAD, C), BF),
            ((M * ROWS * COLS, K * C), BF),
            (flat_weight.shape, BF),
        ],
        mib=18,
        sems=4,
        flops=4 << 30,
        moved=4 << 20,
        away=[((M, G_PAD, C), BF)],
        tie=result,
    )

    def tail(tie):
        return call(
            tail_kernel,
            [FAR] + [VM] * 2 + [FAR],
            [(members_in.shape, BF)],
            (grads, out_grad, far, flat_weight),
            "tail",
            scratch=[
                ((M * ROWS * COLS, K * C), BF),
                (flat_weight.shape, BF),
                (grads.shape, BF),
            ],
            sems=2,
            mib=8,
            flops=2 << 30,
            moved=4 << 20,
            tie=tie,
        )

    weight_grad, in_grad = reduce_gradient(mine, other, tail)
    return (result, in_grad, weight_grad)


def solution(mesh):
    return jax.shard_map(
        shards,
        mesh=mesh,
        in_specs=(P("ens", "lat", "lon", None), P("ens", "lat", "lon", None), P(), P(), P(), P()),
        out_specs=(
            P("ens", "lat", "lon", None),
            P("ens", "lat", "lon", None),
            P(None, "lon", None),
        ),
        check_vma=False,
    )
```
